32 devices in a mesh: tile: 16 (over z, x, core), wave: 2 (over y).
Axes of the slice: x: 2, y: 2, z: 4, core: 2. Of those that a mesh axis runs over, the one named last changes fastest.
Arguments:
- params: float32 [9, 256, 128], P(None, 'tile'), may hold values from -6 to 6
- dual_in: float32 [2, 9, 256, 128], P(None, None, 'tile'), may hold values from -4 to 4
- jacobian: bfloat16 [4, 9, 256, 128], P(None, None, 'tile'), may hold values from -3 to 3
- response: float32 [9, 64], P(None, 'wave'), may hold values from -5 to 5
- observed: bfloat16 [4, 64, 256, 128], P(None, 'wave', 'tile'), may hold values from -6 to 6
- psf: bfloat16 [17, 17], replicated, may hold values from -0.375 to 0.375
- step_size: float32 [], replicated, may hold values from 0.03 to 0.06
- dual_step: float32 [], replicated, may hold values from 0.5 to 1
- tv_bound: float32 [], replicated, may hold values from 1 to 2
- clip_bound: float32 [], replicated, may hold values from 0.5 to 1
Outputs:
- params_out: float32 [9, 256, 128], P(None, 'tile')
- dual_out: float32 [2, 9, 256, 128], P(None, None, 'tile')
- misfit: float32 [], replicated
The draws below stay inside these ranges and needn't reach their ends.
All inputs are finite; a program needn't handle non-finite values.
Results may differ from the reference program's by a relative error of at most 0.0033.
Values may be sent and summed in bfloat16 or wider, within the bound.
A program may use at most 128 MiB of HBM per device.

```python
import jax
import jax.numpy as jnp
from jax import lax

NCOL = 128
NPAR = 9
STOKES = 4
TAPS = 17
NROWS = 256
WAVE = 64


def block_levels(key, shape, shards, least, high):
    gain = 1.0
    for position, shards_of in shards:
        heights = jax.random.uniform(jax.random.fold_in(jax.random.fold_in(key, 6), position), (shards_of,), jnp.float32, least / len(shards), high / len(shards))
        gain = gain * jnp.repeat(jnp.exp(heights), shape[position] // shards_of).reshape((-1,) + (1,) * (len(shape) - 1 - position))
    return gain


def centred(own_key, dims, width, reach, pieces=(), kind=jnp.bfloat16):
    values = width * jax.random.normal(own_key, dims, jnp.float32)
    if pieces:
        values = values * block_levels(own_key, dims, pieces, -0.22, 0.18)
    return jnp.clip(values, -reach, reach).astype(kind)


def setup_inputs(seed: int = 0) -> dict:
    streams_of = jax.random.split(jax.random.key(seed), 11)
    params = centred(streams_of[0], (NPAR, NROWS, NCOL), 1.0, 6.0, ((1, 16),), jnp.float32)
    dual_in = centred(streams_of[1], (2, NPAR, NROWS, NCOL), 0.5, 4.0, ((2, 16),), jnp.float32)
    jacobian = centred(streams_of[2], (STOKES, NPAR, NROWS, NCOL), 0.35, 3.0, ((2, 16),))
    response = centred(streams_of[3], (NPAR, WAVE), 1.0, 5.0, ((1, 2),), jnp.float32)
    observed = centred(streams_of[4], (STOKES, WAVE, NROWS, NCOL), 1.0, 6.0, ((1, 2), (2, 16)))
    psf = centred(streams_of[5], (TAPS, TAPS), (TAPS * TAPS) ** -0.5, 0.375)
    step_size = jnp.clip(jax.random.uniform(streams_of[6], (), jnp.float32, 0.03, 0.06), 0.03, 0.06)
    dual_step = jnp.clip(jax.random.uniform(streams_of[7], (), jnp.float32, 0.5, 1.0), 0.5, 1.0)
    tv_bound = jnp.clip(jax.random.uniform(streams_of[8], (), jnp.float32, 1.0, 2.0), 1.0, 2.0)
    clip_bound = jnp.clip(jax.random.uniform(streams_of[9], (), jnp.float32, 0.5, 1.0), 0.5, 1.0)
    return dict(params=params, dual_in=dual_in, jacobian=jacobian, response=response, observed=observed, psf=psf, step_size=step_size, dual_step=dual_step, tv_bound=tv_bound, clip_bound=clip_bound)


def toeplitz(psf, ncol):
    rows = jnp.arange(ncol, dtype=jnp.int32)[:, None]
    cols = jnp.arange(ncol, dtype=jnp.int32)[None, :]
    offset = (rows - cols + 8) % ncol
    onehot = (offset[None] == jnp.arange(17, dtype=jnp.int32)[:, None, None]).astype(jnp.float32)
    mats = jnp.einsum('ab,bkj->akj', psf.astype(jnp.float32), onehot, precision=lax.Precision.HIGHEST)
    return mats.astype(jnp.bfloat16)


def blur_rows(padded, mats, adjoint):
    count = padded.shape[1] - 16
    total = jnp.zeros((padded.shape[0], count, padded.shape[2]), jnp.float32)
    for tap in range(17):
        window = padded[:, tap:tap + count].astype(jnp.float32)
        if adjoint:
            total = total + jnp.einsum('nrk,jk->nrj', window, mats[16 - tap].astype(jnp.float32), precision=lax.Precision.HIGHEST)
        else:
            total = total + jnp.einsum('nrk,kj->nrj', window, mats[tap].astype(jnp.float32), precision=lax.Precision.HIGHEST)
    return total


def wrap_rows(image):
    return jnp.concatenate([image[:, -8:], image, image[:, :8]], axis=1)


def reference(params, dual_in, jacobian, response, observed, psf, step_size, dual_step, tv_bound, clip_bound):
    mats = toeplitz(psf, params.shape[2])
    grad_r = jnp.roll(params, -1, axis=1) - params
    grad_c = jnp.roll(params, -1, axis=2) - params
    dual_out = jnp.clip(dual_in + dual_step * jnp.stack([grad_r, grad_c]), -tv_bound, tv_bound)
    divergence = (dual_out[0] - jnp.roll(dual_out[0], 1, axis=1)) + (dual_out[1] - jnp.roll(dual_out[1], 1, axis=2))

    def gradient(state):
        def per_stokes(pair):
            jac_one, obs_one = pair
            terms = jac_one.astype(jnp.float32) * state
            synthetic = jnp.einsum('pl,pij->lij', response, terms, precision=lax.Precision.HIGHEST).astype(jnp.bfloat16)
            blurred = blur_rows(wrap_rows(synthetic), mats, False)
            resid = blurred - obs_one.astype(jnp.float32)
            size = jnp.abs(resid)
            huber = jnp.sum(jnp.where(size <= clip_bound, 0.5 * resid * resid, clip_bound * size - 0.5 * clip_bound * clip_bound))
            weighted = jnp.clip(resid, -clip_bound, clip_bound).astype(jnp.bfloat16)
            back = blur_rows(wrap_rows(weighted), mats, True)
            along = jnp.einsum('pl,lij->pij', response, back, precision=lax.Precision.HIGHEST)
            return jac_one.astype(jnp.float32) * along, huber

        parts, hubers = lax.map(per_stokes, (jacobian, observed))
        return jnp.sum(parts, axis=0), jnp.sum(hubers)

    state = params
    misfit = jnp.float32(0.0)
    for step in range(2):
        grad_now, huber = gradient(state)
        if step == 0:
            misfit = huber / (observed.shape[0] * observed.shape[1] * observed.shape[2] * observed.shape[3])
        state = state - step_size * (grad_now - divergence)
    return state, dual_out, misfit
```

```python
import functools

import jax
import jax.numpy as jnp
from jax import lax
from jax.experimental import pallas as pl
from jax.experimental.pallas import tpu as pltpu
from jax.sharding import PartitionSpec as P

MESH = pl.DeviceIdType.MESH
HALO = 8
EDGE = 2 * HALO
TAPS = 17
PAIRS = 9
F32 = jnp.float32
BF16 = jnp.bfloat16


def split_hi_lo(value):
    high = value.astype(BF16).astype(F32)
    return high, value - high


def group_size(count):
    size = 1
    while size * size < count:
        size *= 2
    return size if count % size == 0 else count


def kernel(
    tiles, waves, total_count,
    params_h, dual_h, jac_h, obs_h, response, psf, step_size, dual_step, tv_bound, clip_bound,
    x_out, d_out, m_out,
    params, dual, jac, obs,
    mats, obs_f, jac_f, terms, pairs, proj, acc, xpad, dpad, base, respad, psfpad, rt, rbf, rtb,
    jac_edge, jac_up, jac_dn, par_up, par_dn, dual_up, div_edge, div_up, div_dn,
    full0, edge0, full1, edge1, full0_in, up0_in, dn0_in, full1_in, up1_in, dn1_in,
    m_own, m_mid, m_group, m_cross,
    local, in_send, in_recv, f_send, f_recv, u_send, u_recv, d_send, d_recv,
    mg_send, mg_recv, mc_send, mc_recv,
):
    npar, rows, ncol = params.shape
    images = jac.shape[0]
    stokes = images // npar
    nwave = response.shape[1]
    nimg = stokes * nwave
    width = -(-images // 8) * 8
    wide = -(-images // 16) * 16
    padded = rows + EDGE
    npair = padded // 2
    opair = rows // 2
    me_t = lax.axis_index("tile")
    me_w = lax.axis_index("wave")
    up = lax.rem(me_t + tiles - 1, tiles)
    down = lax.rem(me_t + 1, tiles)
    gsize = group_size(tiles)
    ngroup = tiles // gsize
    my_group = me_t // gsize
    my_place = lax.rem(me_t, gsize)
    spin = [me_w] + [lax.rem(me_w + d, waves) for d in range(1, waves)]
    group_tiles = [me_t]
    group_tiles += [my_group * gsize + lax.rem(my_place + d, gsize) for d in range(1, gsize)]
    group_peers = [(t, w) for i, t in enumerate(group_tiles) for j, w in enumerate(spin) if i + j > 0]
    cross_peers = [
        (lax.rem(my_group + d, ngroup) * gsize + my_place, me_w) for d in range(1, ngroup)
    ]

    barrier = pltpu.get_barrier_semaphore()
    peers = [(t, w) for w in spin for t in (up, down)] + group_peers + cross_peers
    for peer in peers:
        pl.semaphore_signal(barrier, inc=1, device_id=peer, device_id_type=MESH)
    fetch = [
        pltpu.make_async_copy(jac_h, jac, local.at[0]),
        pltpu.make_async_copy(params_h, params, local.at[1]),
        pltpu.make_async_copy(dual_h, dual, local.at[2]),
        pltpu.make_async_copy(obs_h, obs, local.at[3]),
    ]
    for copy in fetch:
        copy.start()
    fetch[0].wait()
    for m in range(images):
        jac_f[m, HALO:HALO + rows, :] = jac[m].astype(F32)
    jac_edge[0] = jac_f[:, HALO:EDGE, :].reshape(images * HALO, ncol).astype(BF16)
    jac_edge[1] = jac_f[:, rows:rows + HALO, :].reshape(images * HALO, ncol).astype(BF16)
    fetch[1].wait()
    fetch[2].wait()
    pl.semaphore_wait(barrier, len(peers))

    def remote(src, dst, send, recv, peer):
        return pltpu.make_async_remote_copy(
            src_ref=src, dst_ref=dst, send_sem=send, recv_sem=recv,
            device_id=peer, device_id_type=MESH,
        )

    above, below = (up, me_w), (down, me_w)
    first = [
        remote(params.at[:, pl.ds(rows - HALO, HALO)], par_up, in_send.at[0], in_recv.at[0], below),
        remote(params.at[:, pl.ds(0, HALO)], par_dn, in_send.at[1], in_recv.at[1], above),
        remote(dual.at[0, :, pl.ds(rows - HALO, HALO)], dual_up, in_send.at[2], in_recv.at[2], below),
        remote(jac_edge.at[1], jac_up, in_send.at[3], in_recv.at[3], below),
        remote(jac_edge.at[0], jac_dn, in_send.at[4], in_recv.at[4], above),
    ]
    for copy in first:
        copy.start()

    step = step_size[0]
    clip = clip_bound[0]
    bound = tv_bound[0]
    dstep = dual_step[0]

    zero_block = jnp.zeros((ncol, ncol), BF16)
    mats[0, ncol:, 0:ncol] = zero_block
    mats[PAIRS - 1, 0:ncol, ncol:] = zero_block
    psfpad[...] = jnp.zeros_like(psfpad)
    psfpad[0:TAPS, 0:TAPS] = psf[...].astype(F32)
    taps = pltpu.roll(psfpad[...], ncol - HALO, 1)
    for tap in range(TAPS):
        line = jnp.broadcast_to(taps[tap:tap + 1, :], (ncol, ncol))
        block = pltpu.roll(line, 0, 1, stride=1, stride_axis=0).astype(BF16)
        if tap % 2 == 0:
            mats[tap // 2, 0:ncol, 0:ncol] = block
            mats[tap // 2, ncol:, ncol:] = block
        else:
            mats[tap // 2, 0:ncol, ncol:] = block
            mats[tap // 2 + 1, ncol:, 0:ncol] = block

    respad[...] = jnp.zeros_like(respad)
    respad[0:npar, 0:nwave] = response[...]
    rt[...] = jnp.zeros_like(rt)
    spread = respad[...]
    for s in range(stokes):
        shifted = spread if s == 0 else pltpu.roll(spread, s * nwave, 1)
        for part in range(3):
            at = part * width + s * npar
            rt[at:at + npar, :] = shifted[0:npar]
    full = rt[...]
    high, low = split_hi_lo(full)
    place = lax.broadcasted_iota(jnp.int32, full.shape, 0)
    rbf[...] = jnp.where(place < 2 * width, high, low).T.astype(BF16)
    rtb[...] = jnp.concatenate([high[0:width], low[0:width]], axis=0).astype(BF16)

    for m in range(images, width):
        terms[m * padded:(m + 1) * padded, :] = jnp.zeros((padded, ncol), F32)
    d1 = params[...]
    xpad[:, HALO:HALO + rows, :] = d1
    d1 = pltpu.roll(d1, ncol - 1, 2) - d1
    d1 = jnp.clip(dual[1] + dstep * d1, -bound, bound)
    d_out[1] = d1
    fetch[3].wait()
    obs_f[...] = obs[...].astype(F32).reshape(nimg * rows, ncol)

    for copy in first:
        copy.wait()
    xpad[:, 0:HALO, :] = par_up[...]
    xpad[:, HALO + rows:, :] = par_dn[...]
    d0 = xpad[:, HALO + 1:HALO + 1 + rows, :] - xpad[:, HALO:HALO + rows, :]
    d0 = jnp.clip(dual[0] + dstep * d0, -bound, bound)
    d_out[0] = d0
    side = xpad[:, 1:HALO + 1, :] - xpad[:, 0:HALO, :]
    dpad[:, 0:HALO, :] = jnp.clip(dual_up[...] + dstep * side, -bound, bound)
    dpad[:, HALO:, :] = d0
    div = (d0 - dpad[:, HALO - 1:HALO - 1 + rows, :]) + (d1 - pltpu.roll(d1, 1, 2))
    base[:, HALO:HALO + rows, :] = div
    div_edge[0] = div[:, 0:HALO, :]
    div_edge[1] = div[:, rows - HALO:, :]
    copies_v = [
        remote(div_edge.at[1], div_up, in_send.at[5], in_recv.at[5], below),
        remote(div_edge.at[0], div_dn, in_send.at[6], in_recv.at[6], above),
    ]
    for copy in copies_v:
        copy.start()
    jac_f[:, 0:HALO, :] = jac_up[...].astype(F32).reshape(images, HALO, ncol)
    jac_f[:, HALO + rows:, :] = jac_dn[...].astype(F32).reshape(images, HALO, ncol)

    zero_k = jnp.zeros((rbf.shape[1] - 3 * width, 2 * ncol), F32)

    def widen(value):
        if wide == width:
            return value.astype(BF16)
        fill = jnp.zeros((wide - width, value.shape[1]), F32)
        return jnp.concatenate([value, fill], axis=0).astype(BF16)

    for it in range(2):
        for m in range(images):
            terms[m * padded:(m + 1) * padded, :] = jac_f[m] * xpad[m % npar]
        for q in range(npair):
            for i in range(2):
                value = terms[pl.ds(2 * q + i, width, stride=padded), :]
                value = jnp.concatenate(split_hi_lo(value), axis=0).astype(BF16)
                pairs[q * 2 * width:(q + 1) * 2 * width, i * ncol:(i + 1) * ncol] = value
        total = None
        for k in range(PAIRS):
            window = pairs[k * 2 * width:(k + opair) * 2 * width, :]
            part = lax.dot_general(
                window, mats[k], (((1,), (1,)), ((), ())), preferred_element_type=F32
            )
            total = part if total is None else total + part
        loss = jnp.zeros((8, ncol), F32)
        for r in range(opair):
            both = total[r * 2 * width:(r + 1) * 2 * width]
            bhi, blo = split_hi_lo(both[:width] + both[width:])
            stack = jnp.concatenate([bhi, blo, bhi, zero_k], axis=0).astype(BF16)
            blurred = jnp.dot(rbf[...], stack, preferred_element_type=F32)
            halves = []
            for i in range(2):
                target = obs_f[pl.ds(2 * r + i, nimg, stride=rows), :]
                resid = blurred[:, i * ncol:(i + 1) * ncol] - target
                held = jnp.clip(resid, -clip, clip)
                if it == 0:
                    huber = held * (resid - 0.5 * held)
                    loss = loss + jnp.sum(huber.reshape(nimg // 8, 8, ncol), axis=0)
                halves.append(held.astype(BF16))
            weighted = jnp.concatenate(halves, axis=1)
            both = jnp.dot(rtb[...], weighted, preferred_element_type=F32)
            proj[r * wide:(r + 1) * wide, :] = widen(both[:width] + both[width:])
        if it == 0:
            m_own[...] = loss
            slot = my_place * waves + me_w
            m_group[slot] = loss
            copies_g = [
                remote(m_own, m_group.at[slot], mg_send.at[d], mg_recv.at[d], peer)
                for d, peer in enumerate(group_peers)
            ]
            for copy in copies_g:
                copy.start()
        for k in range(PAIRS):
            back = jnp.dot(proj[...], mats[k], preferred_element_type=F32)
            for q in range(opair):
                part = back[q * wide:(q + 1) * wide]
                at = (k + q) * wide
                if k == 0 or q == opair - 1:
                    acc[at:at + wide, :] = part
                else:
                    acc[at:at + wide, :] += part
        for q in range(npair):
            for i in range(2):
                value = acc[q * wide:q * wide + width, i * ncol:(i + 1) * ncol]
                terms[pl.ds(2 * q + i, width, stride=padded), :] = value
        grads = []
        for p in range(npar):
            grad = None
            for s in range(stokes):
                m = s * npar + p
                part = jac_f[m] * terms[m * padded:(m + 1) * padded, :]
                grad = part if grad is None else grad + part
            grads.append(grad)
        reach = EDGE if it == 0 else HALO
        whole = grads if it == 0 else [g[HALO:HALO + rows] for g in grads]
        whole = jnp.concatenate(whole, axis=0).astype(BF16)
        full_out, edge_out = (full0, edge0) if it == 0 else (full1, edge1)
        full_in, up_in, dn_in = (full0_in, up0_in, dn0_in) if it == 0 else (full1_in, up1_in, dn1_in)
        edge_out[0] = jnp.concatenate([g[:reach] for g in grads], axis=0).astype(BF16)
        edge_out[1] = jnp.concatenate([g[padded - reach:] for g in grads], axis=0).astype(BF16)
        full_out[...] = whole
        full_in[me_w] = whole
        copies = []
        for d in range(waves - 1, -1, -1):
            copies += [
                remote(edge_out.at[1], up_in.at[me_w], u_send.at[it, d], u_recv.at[it, d], (down, spin[d])),
                remote(edge_out.at[0], dn_in.at[me_w], d_send.at[it, d], d_recv.at[it, d], (up, spin[d])),
            ]
        for d in range(1, waves):
            copies.append(
                remote(full_out, full_in.at[me_w], f_send.at[it, d], f_recv.at[it, d], (me_t, spin[d]))
            )
        for copy in copies:
            copy.start()
        if it == 0:
            for copy in copies_v:
                copy.wait()
            base[:, 0:HALO, :] = div_up[...]
            base[:, HALO + rows:, :] = div_dn[...]
            base[...] = xpad[...] + step * base[...]
        for copy in copies:
            copy.wait()

        def added(ref, count):
            value = ref[0].astype(F32)
            for w in range(1, waves):
                value = value + ref[w].astype(F32)
            return value.reshape(npar, count, ncol)

        span = padded if it == 0 else rows
        inner = added(full_in, span)
        top = inner[:, :reach] + added(up_in, reach)
        low = inner[:, span - reach:] + added(dn_in, reach)
        if it == 0:
            kept = [base[:, :reach, :] - step * top]
            if span > 2 * reach:
                kept.append(base[:, reach:span - reach, :] - step * inner[:, reach:span - reach])
            kept.append(base[:, span - reach:, :] - step * low)
            mid = base[:, HALO:HALO + rows, :] - xpad[:, HALO:HALO + rows, :]
            at = 0
            for value in kept:
                xpad[:, at:at + value.shape[1], :] = value
                at += value.shape[1]
            base[:, HALO:HALO + rows, :] = xpad[:, HALO:HALO + rows, :] + mid
            for copy in copies_g:
                copy.wait()
            total_m = m_group[0]
            for g in range(1, gsize * waves):
                total_m = total_m + m_group[g]
            m_mid[...] = total_m
            m_cross[my_group] = total_m
            copies_c = [
                remote(m_mid, m_cross.at[my_group], mc_send.at[d], mc_recv.at[d], peer)
                for d, peer in enumerate(cross_peers)
            ]
            for copy in copies_c:
                copy.start()
        else:
            x_out[:, 0:reach, :] = base[:, HALO:HALO + reach, :] - step * top
            if span > 2 * reach:
                x_out[:, reach:span - reach, :] = (
                    base[:, HALO + reach:HALO + span - reach, :] - step * inner[:, reach:span - reach]
                )
            x_out[:, span - reach:, :] = base[:, HALO + span - reach:HALO + span, :] - step * low
            for copy in copies_c:
                copy.wait()
            tot = m_cross[0]
            for g in range(1, ngroup):
                tot = tot + m_cross[g]
            m_out[...] = jnp.full((8, ncol), jnp.sum(tot) / total_count, F32)


def hand_out(x, d, m, x_h, d_h, m_s, sem):
    copies = [pltpu.make_async_copy(x, x_h, sem.at[0]), pltpu.make_async_copy(d, d_h, sem.at[1])]
    for copy in copies:
        copy.start()
    m_s[0] = m[0, 0]
    for copy in copies:
        copy.wait()


def per_device(
    params, dual_in, jacobian, response, observed, psf, step_size, dual_step, tv_bound, clip_bound
):
    stokes, nwave, rows, ncol = observed.shape
    npar = params.shape[0]
    nimg = stokes * nwave
    images = stokes * npar
    width = -(-images // 8) * 8
    wide = -(-images // 16) * 16
    kdim = -(-3 * width // 128) * 128
    padded = rows + EDGE
    npair = padded // 2
    opair = rows // 2
    tiles = lax.axis_size("tile")
    waves = lax.axis_size("wave")
    total_count = float(nimg * waves * rows * tiles * ncol)
    gsize = group_size(tiles)
    ngroup = tiles // gsize
    vmem = pl.BlockSpec(memory_space=pltpu.VMEM)
    smem = pl.BlockSpec(memory_space=pltpu.SMEM)
    hbm = pl.BlockSpec(memory_space=pltpu.HBM)
    dma = pltpu.SemaphoreType.DMA
    state, dual_out, misfit = pl.pallas_call(
        functools.partial(kernel, tiles, waves, total_count),
        out_shape=(
            pltpu.VMEM((npar, rows, ncol), F32),
            pltpu.VMEM((2, npar, rows, ncol), F32),
            pltpu.VMEM((8, ncol), F32),
        ),
        in_specs=[hbm] * 4 + [vmem] * 2 + [smem] * 4,
        out_specs=(vmem, vmem, vmem),
        scratch_shapes=[
            pltpu.VMEM((npar, rows, ncol), F32),
            pltpu.VMEM((2, npar, rows, ncol), F32),
            pltpu.VMEM((images, rows, ncol), BF16),
            pltpu.VMEM((nimg, rows, ncol), BF16),
            pltpu.VMEM((PAIRS, 2 * ncol, 2 * ncol), BF16),
            pltpu.VMEM((nimg * rows, ncol), F32),
            pltpu.VMEM((images, padded, ncol), F32),
            pltpu.VMEM((width * padded, ncol), F32),
            pltpu.VMEM((npair * 2 * width, 2 * ncol), BF16),
            pltpu.VMEM((opair * wide, 2 * ncol), BF16),
            pltpu.VMEM((npair * wide, 2 * ncol), F32),
            pltpu.VMEM((npar, padded, ncol), F32),
            pltpu.VMEM((npar, rows + HALO, ncol), F32),
            pltpu.VMEM((npar, padded, ncol), F32),
            pltpu.VMEM((-(-npar // 8) * 8, nimg), F32),
            pltpu.VMEM((-(-TAPS // 8) * 8, ncol), F32),
            pltpu.VMEM((kdim, nimg), F32),
            pltpu.VMEM((nimg, kdim), BF16),
            pltpu.VMEM((2 * width, nimg), BF16),
            pltpu.VMEM((2, images * HALO, ncol), BF16),
            pltpu.VMEM((images * HALO, ncol), BF16),
            pltpu.VMEM((images * HALO, ncol), BF16),
            pltpu.VMEM((npar, HALO, ncol), F32),
            pltpu.VMEM((npar, HALO, ncol), F32),
            pltpu.VMEM((npar, HALO, ncol), F32),
            pltpu.VMEM((2, npar, HALO, ncol), F32),
            pltpu.VMEM((npar, HALO, ncol), F32),
            pltpu.VMEM((npar, HALO, ncol), F32),
            pltpu.VMEM((npar * padded, ncol), BF16),
            pltpu.VMEM((2, npar * EDGE, ncol), BF16),
            pltpu.VMEM((npar * rows, ncol), BF16),
            pltpu.VMEM((2, npar * HALO, ncol), BF16),
            pltpu.VMEM((waves, npar * padded, ncol), BF16),
            pltpu.VMEM((waves, npar * EDGE, ncol), BF16),
            pltpu.VMEM((waves, npar * EDGE, ncol), BF16),
            pltpu.VMEM((waves, npar * rows, ncol), BF16),
            pltpu.VMEM((waves, npar * HALO, ncol), BF16),
            pltpu.VMEM((waves, npar * HALO, ncol), BF16),
            pltpu.VMEM((8, ncol), F32),
            pltpu.VMEM((8, ncol), F32),
            pltpu.VMEM((gsize * waves, 8, ncol), F32),
            pltpu.VMEM((ngroup, 8, ncol), F32),
            dma((5,)),
            dma((7,)), dma((7,)),
            dma((2, waves)), dma((2, waves)),
            dma((2, waves)), dma((2, waves)),
            dma((2, waves)), dma((2, waves)),
            dma((gsize * waves,)), dma((gsize * waves,)),
            dma((ngroup,)), dma((ngroup,)),
        ],
        compiler_params=pltpu.CompilerParams(
            collective_id=0, has_side_effects=True, vmem_limit_bytes=66_000_000
        ),
    )(
        params, dual_in, jacobian.reshape(images, rows, ncol),
        observed.reshape(nimg, rows, ncol), response, psf,
        step_size.reshape(1), dual_step.reshape(1), tv_bound.reshape(1), clip_bound.reshape(1),
    )
    state, dual_out, misfit = pl.pallas_call(
        hand_out,
        out_shape=(
            jax.ShapeDtypeStruct((npar, rows, ncol), F32),
            jax.ShapeDtypeStruct((2, npar, rows, ncol), F32),
            jax.ShapeDtypeStruct((1,), F32),
        ),
        in_specs=[vmem] * 3,
        out_specs=(hbm, hbm, smem),
        scratch_shapes=[dma((2,))],
        compiler_params=pltpu.CompilerParams(vmem_limit_bytes=1_000_000),
    )(state, dual_out, misfit)
    return state, dual_out, misfit.reshape(())


def solution(mesh):
    in_specs = (
        P(None, "tile", None),
        P(None, None, "tile", None),
        P(None, None, "tile", None),
        P(None, "wave"),
        P(None, "wave", "tile", None),
        P(),
        P(),
        P(),
        P(),
        P(),
    )
    out_specs = (P(None, "tile", None), P(None, None, "tile", None), P())
    return jax.shard_map(
        per_device, mesh=mesh, in_specs=in_specs, out_specs=out_specs, check_vma=False
    )
```

```python
import functools

import jax
import jax.numpy as jnp
from jax import lax
from jax.experimental import pallas as pl
from jax.experimental.pallas import tpu as pltpu
from jax.sharding import PartitionSpec as P

MESH = pl.DeviceIdType.MESH
HALO = 8
TAPS = 17
F32 = jnp.float32
BF16 = jnp.bfloat16


def split_hi_lo(value):
    high = value.astype(BF16).astype(F32)
    return high, value - high


def group_size(count):
    size = 1
    while size * size < count:
        size *= 2
    return size if count % size == 0 else count


def kernel(
    tiles, waves, total_count,
    params_h, dual_h, jac_h, obs_h, response, psf, step_size, dual_step, tv_bound, clip_bound,
    x_out, d_out, m_out,
    params, dual, jac, obs,
    wt, main_a, half_a, obs_f, obs_l, jac_n, jac_l, x_l, lhs, tot, proj, prod, grad_c,
    x_c, div_c, base_c, div_n, dpad, respad, psfpad, rt, rbf, rtb,
    jac_edge, jac_up, jac_dn, row_dn, row_up, row_above, row_below,
    full0, edge0, full1, edge1, full0_in, up0_in, dn0_in, full1_in, up1_in, dn1_in,
    m_own, m_mid, m_group, m_cross,
    local, in_send, in_recv, f_send, f_recv, u_send, u_recv, d_send, d_recv,
    mg_send, mg_recv, mc_send, mc_recv,
):
    npar, rows, ncol = params.shape
    images = jac.shape[0]
    stokes = images // npar
    nwave = response.shape[1]
    nimg = stokes * nwave
    width = -(-images // 8) * 8
    wide = -(-images // 16) * 16
    nrg = rows // HALO
    span = nrg + 2
    blk = HALO
    cols = ncol // blk
    unit = npar * blk
    half_rows = 16 * -(-npar // 16)
    me_t = lax.axis_index("tile")
    me_w = lax.axis_index("wave")
    up = lax.rem(me_t + tiles - 1, tiles)
    down = lax.rem(me_t + 1, tiles)
    gsize = group_size(tiles)
    ngroup = tiles // gsize
    my_group = me_t // gsize
    my_place = lax.rem(me_t, gsize)
    spin = [me_w] + [lax.rem(me_w + d, waves) for d in range(1, waves)]
    group_tiles = [me_t]
    group_tiles += [my_group * gsize + lax.rem(my_place + d, gsize) for d in range(1, gsize)]
    group_peers = [(t, w) for i, t in enumerate(group_tiles) for j, w in enumerate(spin) if i + j > 0]
    cross_peers = [
        (lax.rem(my_group + d, ngroup) * gsize + my_place, me_w) for d in range(1, ngroup)
    ]

    barrier = pltpu.get_barrier_semaphore()
    peers = [(up, me_w), (down, me_w)] + group_peers + cross_peers
    for peer in peers:
        pl.semaphore_signal(barrier, inc=1, device_id=peer, device_id_type=MESH)
    fetch = [
        pltpu.make_async_copy(jac_h, jac, local.at[0]),
        pltpu.make_async_copy(params_h, params, local.at[1]),
        pltpu.make_async_copy(dual_h, dual, local.at[2]),
        pltpu.make_async_copy(obs_h, obs, local.at[3]),
    ]
    for copy in fetch:
        copy.start()

    lane = lax.broadcasted_iota(jnp.int32, (1, ncol), 1)
    group_bit = [(lane // (cols << b)) % 2 == 0 for b in range(3)]
    near = lane % cols < HALO

    def swap_blocks(parts):
        parts = list(parts)
        for b in range(3):
            k = 1 << b
            shift = cols * k
            for i in range(blk):
                if i & k:
                    continue
                one, two = parts[i], parts[i + k]
                parts[i] = jnp.where(group_bit[b], one, pltpu.roll(two, shift, 1))
                parts[i + k] = jnp.where(group_bit[b], pltpu.roll(one, ncol - shift, 1), two)
        return parts

    def image_rows(rg, b):
        return slice((rg * blk + b) * width, (rg * blk + b + 1) * width)

    def unit_rows(rg, b):
        return slice((rg * blk + b) * npar, (rg * blk + b + 1) * npar)

    def to_units(source, target, rg_from, rg_to):
        parts = swap_blocks([source[:, rg_from * HALO + r, :] for r in range(HALO)])
        for b in range(blk):
            target[unit_rows(rg_to, b), :] = parts[b]

    jac_n[images * rows:, :] = jnp.zeros((jac_n.shape[0] - images * rows, ncol), F32)
    fetch[0].wait()
    for m in range(images):
        jac_n[m * rows:(m + 1) * rows, :] = jac[m].astype(F32)
    for rg in range(nrg):
        for g in range(width // 8):
            parts = swap_blocks(
                [jac_n[pl.ds(g * 8 * rows + rg * HALO + r, 8, stride=rows), :] for r in range(HALO)]
            )
            for b in range(blk):
                at = ((rg + 1) * blk + b) * width + g * 8
                jac_l[at:at + 8, :] = parts[b]
    jac_edge[0] = jac_l[blk * width:2 * blk * width, :].astype(BF16)
    jac_edge[1] = jac_l[nrg * blk * width:(nrg + 1) * blk * width, :].astype(BF16)
    fetch[1].wait()
    for rg in range(nrg):
        to_units(params, x_c, rg, rg + 1)
    fetch[2].wait()
    row_dn[...] = jnp.zeros_like(row_dn)
    row_up[...] = jnp.zeros_like(row_up)
    row_dn[0:npar, :] = params[:, rows - 1, :]
    row_dn[half_rows:half_rows + npar, :] = dual[0, :, rows - 1, :]
    row_up[0:npar, :] = params[:, 0, :]
    pl.semaphore_wait(barrier, len(peers))

    def remote(src, dst, send, recv, peer):
        return pltpu.make_async_remote_copy(
            src_ref=src, dst_ref=dst, send_sem=send, recv_sem=recv,
            device_id=peer, device_id_type=MESH,
        )

    above, below = (up, me_w), (down, me_w)

    def unit_span(rg, count):
        return pl.ds(rg * unit, count * unit)

    first = [
        remote(row_dn, row_above, in_send.at[0], in_recv.at[0], below),
        remote(row_up, row_below, in_send.at[1], in_recv.at[1], above),
        remote(jac_edge.at[1], jac_up, in_send.at[2], in_recv.at[2], below),
        remote(jac_edge.at[0], jac_dn, in_send.at[3], in_recv.at[3], above),
        remote(x_c.at[unit_span(nrg, 1)], x_c.at[unit_span(0, 1)], in_send.at[4], in_recv.at[4], below),
        remote(x_c.at[unit_span(1, 1)], x_c.at[unit_span(nrg + 1, 1)], in_send.at[5], in_recv.at[5], above),
    ]
    for copy in first:
        copy.start()

    step = step_size[0]
    clip = clip_bound[0]
    bound = tv_bound[0]
    dstep = dual_step[0]

    psfpad[...] = jnp.zeros_like(psfpad)
    psfpad[0:TAPS, 0:TAPS] = psf[...].astype(F32)
    taps = pltpu.roll(psfpad[...], ncol - HALO, 1)
    for tap in range(TAPS):
        line = jnp.broadcast_to(taps[tap:tap + 1, :], (cols, ncol))
        line = pltpu.roll(line, 0, 1, stride=1, stride_axis=0)
        side = jnp.where(near, pltpu.roll(line, ncol - cols, 1), pltpu.roll(line, cols, 1))
        for ref, value in ((main_a, line), (half_a, side)):
            value = jnp.where(lane < cols, value, 0.0)
            for b in range(3):
                value = value + pltpu.roll(value, cols << b, 1)
            ref[tap * cols:(tap + 1) * cols, :] = value
    edge1[...] = jnp.zeros_like(edge1)
    wt[0, ncol:, :] = jnp.zeros((wt.shape[1] - ncol, 2 * ncol), BF16)
    for rg in range(1, span):
        for ro in range(nrg):
            if not 0 <= rg - ro <= 2:
                wt[rg, ro * ncol:(ro + 1) * ncol, :] = jnp.zeros((ncol, 2 * ncol), BF16)
    for delta in range(3):
        for r in range(HALO):
            for part, ref in ((0, main_a), (1, half_a)):
                value = jnp.zeros((cols, ncol), F32)
                for kr in range(HALO):
                    tap = delta * HALO + kr - r
                    if 0 <= tap < TAPS:
                        value = jnp.where(lane // cols == kr, ref[tap * cols:(tap + 1) * cols, :], value)
                value = value.astype(BF16)
                for ro in range(nrg):
                    at = ro * ncol + r * cols
                    wt[ro + delta, at:at + cols, part * ncol:(part + 1) * ncol] = value

    def expand(rg):
        for b in range(blk):
            value = x_c[unit_rows(rg, b), :]
            at = (rg * blk + b) * width
            for s in range(stokes):
                x_l[at + s * npar:at + (s + 1) * npar, :] = value

    def build(rg):
        terms = [jac_l[image_rows(rg, b), :] * x_l[image_rows(rg, b), :] for b in range(blk)]
        for b in range(blk):
            side = jnp.where(near, terms[(b + 1) % blk], terms[(b + blk - 1) % blk])
            at = (rg * blk + b) * 2 * width
            for part, value in ((0, terms[b]), (1, side)):
                value = jnp.concatenate(split_hi_lo(value), axis=0).astype(BF16)
                lhs[at:at + 2 * width, part * ncol:(part + 1) * ncol] = value

    def forward(rg):
        window = lhs[rg * blk * 2 * width:(rg + 1) * blk * 2 * width, :]
        return lax.dot_general(
            window, wt[rg], (((1,), (1,)), ((), ())), preferred_element_type=F32
        )

    if width > images:
        for rg in range(span):
            for b in range(blk):
                at = (rg * blk + b) * width
                x_l[at + images:at + width, :] = jnp.zeros((width - images, ncol), F32)
    for rg in range(1, nrg + 1):
        expand(rg)
        build(rg)
    own = None
    for rg in range(1, nrg + 1):
        part = forward(rg)
        own = part if own is None else own + part
    tot[...] = own

    respad[...] = jnp.zeros_like(respad)
    respad[0:npar, 0:nwave] = response[...]
    rt[...] = jnp.zeros_like(rt)
    spread = respad[...]
    for s in range(stokes):
        shifted = spread if s == 0 else pltpu.roll(spread, s * nwave, 1)
        for part in range(3):
            at = part * width + s * npar
            rt[at:at + npar, :] = shifted[0:npar]
    full = rt[...]
    high, low = split_hi_lo(full)
    place = lax.broadcasted_iota(jnp.int32, full.shape, 0)
    rbf[...] = jnp.where(place < 2 * width, high, low).T.astype(BF16)
    rtb[...] = jnp.concatenate([high[0:width], low[0:width]], axis=0).astype(BF16)

    d1 = params[...]
    d1 = pltpu.roll(d1, ncol - 1, 2) - d1
    d1 = jnp.clip(dual[1] + dstep * d1, -bound, bound)
    d_out[1] = d1
    fetch[3].wait()
    obs_f[...] = obs[...].astype(F32).reshape(nimg * rows, ncol)
    for g in range(nimg // 8):
        for rg in range(nrg):
            parts = swap_blocks(
                [obs_f[pl.ds(g * 8 * rows + rg * HALO + r, 8, stride=rows), :] for r in range(HALO)]
            )
            for b in range(blk):
                at = b * nimg + g * 8
                obs_l[at:at + 8, rg * ncol:(rg + 1) * ncol] = parts[b]

    for copy in first[:2]:
        copy.wait()
    now = params[...]
    dpad[:, HALO:HALO + rows, :] = now
    dpad[:, HALO + rows, :] = row_below[0:npar, :]
    d0 = dpad[:, HALO + 1:HALO + 1 + rows, :] - now
    d0 = jnp.clip(dual[0] + dstep * d0, -bound, bound)
    d_out[0] = d0
    side = params[:, 0, :] - row_above[0:npar, :]
    side = jnp.clip(row_above[half_rows:half_rows + npar, :] + dstep * side, -bound, bound)
    dpad[:, HALO - 1, :] = side
    dpad[:, HALO:HALO + rows, :] = d0
    div_n[...] = (d0 - dpad[:, HALO - 1:HALO - 1 + rows, :]) + (d1 - pltpu.roll(d1, 1, 2))
    for rg in range(nrg):
        to_units(div_n, div_c, rg, rg + 1)
    copies_v = [
        remote(div_c.at[unit_span(nrg, 1)], div_c.at[unit_span(0, 1)], in_send.at[6], in_recv.at[6], below),
        remote(div_c.at[unit_span(1, 1)], div_c.at[unit_span(nrg + 1, 1)], in_send.at[7], in_recv.at[7], above),
    ]
    for copy in copies_v:
        copy.start()
    for copy in first[2:]:
        copy.wait()
    jac_l[0:blk * width, :] = jac_up[...].astype(F32)
    jac_l[(nrg + 1) * blk * width:, :] = jac_dn[...].astype(F32)
    zero_k = jnp.zeros((rbf.shape[1] - 3 * width, nrg * ncol), F32)

    def widen(value):
        if wide == width:
            return value.astype(BF16)
        fill = jnp.zeros((wide - width, value.shape[1]), F32)
        return jnp.concatenate([value, fill], axis=0).astype(BF16)

    for it in range(2):
        for rg in (0, nrg + 1) if it == 0 else range(span):
            expand(rg)
            build(rg)
        if it == 0:
            total = tot[...] + forward(0) + forward(nrg + 1)
        else:
            total = None
            for rg in range(span):
                part = forward(rg)
                total = part if total is None else total + part
        loss = jnp.zeros((8, nrg * ncol), F32)
        for b in range(blk):
            both = total[b * 2 * width:(b + 1) * 2 * width]
            bhi, blo = split_hi_lo(both[:width] + both[width:])
            stack = jnp.concatenate([bhi, blo, bhi, zero_k], axis=0).astype(BF16)
            blurred = jnp.dot(rbf[...], stack, preferred_element_type=F32)
            resid = blurred - obs_l[b * nimg:(b + 1) * nimg, :]
            held = jnp.clip(resid, -clip, clip)
            if it == 0:
                huber = held * (resid - 0.5 * held)
                loss = loss + jnp.sum(huber.reshape(nimg // 8, 8, nrg * ncol), axis=0)
            both = jnp.dot(rtb[...], held.astype(BF16), preferred_element_type=F32)
            proj[b * wide:(b + 1) * wide, :] = widen(both[:width] + both[width:])
        if it == 0:
            loss = sum(loss[:, i * ncol:(i + 1) * ncol] for i in range(nrg))
            m_own[...] = loss
            slot = my_place * waves + me_w
            m_group[slot] = loss
            copies_g = [
                remote(m_own, m_group.at[slot], mg_send.at[d], mg_recv.at[d], peer)
                for d, peer in enumerate(group_peers)
            ]
            for copy in copies_g:
                copy.start()
        for rg in range(span):
            back = jnp.dot(proj[...], wt[rg], preferred_element_type=F32)
            mains = [back[b * wide:b * wide + width, 0:ncol] for b in range(blk)]
            sides = [back[b * wide:b * wide + width, ncol:] for b in range(blk)]
            for b in range(blk):
                along = mains[b] + jnp.where(near, sides[(b + blk - 1) % blk], sides[(b + 1) % blk])
                at = (rg * blk + b) * width
                prod[at:at + width, :] = jac_l[at:at + width, :] * along
                grad = None
                for s in range(stokes):
                    part = prod[at + s * npar:at + (s + 1) * npar, :]
                    grad = part if grad is None else grad + part
                grad_c[unit_rows(rg, b), :] = grad
        reach = 2 * unit if it == 0 else unit
        size = span * unit
        start = 0 if it == 0 else unit
        full_out, edge_out = (full0, edge0) if it == 0 else (full1, edge1)
        full_in, up_in, dn_in = (full0_in, up0_in, dn0_in) if it == 0 else (full1_in, up1_in, dn1_in)
        edge_out[0, 0:reach, :] = grad_c[0:reach, :].astype(BF16)
        edge_out[1, 0:reach, :] = grad_c[size - reach:, :].astype(BF16)
        whole = grad_c[start:size - start, :].astype(BF16)
        full_out[...] = whole
        full_in[me_w] = whole
        copies = []
        for d in range(waves - 1, -1, -1):
            copies += [
                remote(edge_out.at[1], up_in.at[me_w], u_send.at[it, d], u_recv.at[it, d], (down, spin[d])),
                remote(edge_out.at[0], dn_in.at[me_w], d_send.at[it, d], d_recv.at[it, d], (up, spin[d])),
            ]
        for d in range(1, waves):
            copies.append(
                remote(full_out, full_in.at[me_w], f_send.at[it, d], f_recv.at[it, d], (me_t, spin[d]))
            )
        for copy in copies:
            copy.start()
        if it == 0:
            for copy in copies_v:
                copy.wait()
            base_c[...] = x_c[...] + step * div_c[...]
        else:
            base_c[unit:size - unit, :] = x_c[unit:size - unit, :] + step * div_c[unit:size - unit, :]
            for copy in copies_g:
                copy.wait()
            total_m = m_group[0]
            for g in range(1, gsize * waves):
                total_m = total_m + m_group[g]
            m_mid[...] = total_m
            m_cross[my_group] = total_m
            copies_c = [
                remote(m_mid, m_cross.at[my_group], mc_send.at[d], mc_recv.at[d], peer)
                for d, peer in enumerate(cross_peers)
            ]
            for copy in copies_c:
                copy.start()
        for copy in copies:
            copy.wait()

        def added(ref, count):
            value = ref[0, 0:count, :].astype(F32)
            for w in range(1, waves):
                value = value + ref[w, 0:count, :].astype(F32)
            return value

        inner = added(full_in, size - 2 * start)
        top = inner[:reach] + added(up_in, reach)
        low = inner[size - 2 * start - reach:] + added(dn_in, reach)
        end = size - start
        x_c[start:start + reach, :] = base_c[start:start + reach, :] - step * top
        if end - start > 2 * reach:
            x_c[start + reach:end - reach, :] = (
                base_c[start + reach:end - reach, :] - step * inner[reach:end - start - reach]
            )
        x_c[end - reach:end, :] = base_c[end - reach:end, :] - step * low
    for rg in range(nrg):
        parts = swap_blocks([x_c[unit_rows(rg + 1, b), :] for b in range(blk)])
        for r in range(HALO):
            x_out[:, rg * HALO + r, :] = parts[r]
    for copy in copies_c:
        copy.wait()
    tot_m = m_cross[0]
    for g in range(1, ngroup):
        tot_m = tot_m + m_cross[g]
    m_out[...] = jnp.full((8, ncol), jnp.sum(tot_m) / total_count, F32)


def hand_out(x, d, m, x_h, d_h, m_s, sem):
    copies = [pltpu.make_async_copy(x, x_h, sem.at[0]), pltpu.make_async_copy(d, d_h, sem.at[1])]
    for copy in copies:
        copy.start()
    m_s[0] = m[0, 0]
    for copy in copies:
        copy.wait()


def per_device(
    params, dual_in, jacobian, response, observed, psf, step_size, dual_step, tv_bound, clip_bound
):
    stokes, nwave, rows, ncol = observed.shape
    npar = params.shape[0]
    nimg = stokes * nwave
    images = stokes * npar
    width = -(-images // 8) * 8
    wide = -(-images // 16) * 16
    kdim = -(-3 * width // 128) * 128
    nrg = rows // HALO
    span = nrg + 2
    blk = HALO
    cols = ncol // blk
    unit = npar * blk
    edge = -(-unit // 16) * 16
    half_rows = 16 * -(-npar // 16)
    tiles = lax.axis_size("tile")
    waves = lax.axis_size("wave")
    total_count = float(nimg * waves * rows * tiles * ncol)
    gsize = group_size(tiles)
    ngroup = tiles // gsize
    vmem = pl.BlockSpec(memory_space=pltpu.VMEM)
    smem = pl.BlockSpec(memory_space=pltpu.SMEM)
    hbm = pl.BlockSpec(memory_space=pltpu.HBM)
    dma = pltpu.SemaphoreType.DMA
    state, dual_out, misfit = pl.pallas_call(
        functools.partial(kernel, tiles, waves, total_count),
        out_shape=(
            pltpu.VMEM((npar, rows, ncol), F32),
            pltpu.VMEM((2, npar, rows, ncol), F32),
            pltpu.VMEM((8, ncol), F32),
        ),
        in_specs=[hbm] * 4 + [vmem] * 2 + [smem] * 4,
        out_specs=(vmem, vmem, vmem),
        scratch_shapes=[
            pltpu.VMEM((npar, rows, ncol), F32),
            pltpu.VMEM((2, npar, rows, ncol), F32),
            pltpu.VMEM((images, rows, ncol), BF16),
            pltpu.VMEM((nimg, rows, ncol), BF16),
            pltpu.VMEM((span, nrg * ncol, 2 * ncol), BF16),
            pltpu.VMEM((TAPS * cols, ncol), F32),
            pltpu.VMEM((TAPS * cols, ncol), F32),
            pltpu.VMEM((nimg * rows, ncol), F32),
            pltpu.VMEM((blk * nimg, nrg * ncol), F32),
            pltpu.VMEM((width * rows, ncol), F32),
            pltpu.VMEM((span * blk * width, ncol), F32),
            pltpu.VMEM((span * blk * width, ncol), F32),
            pltpu.VMEM((span * blk * 2 * width, 2 * ncol), BF16),
            pltpu.VMEM((blk * 2 * width, nrg * ncol), F32),
            pltpu.VMEM((blk * wide, nrg * ncol), BF16),
            pltpu.VMEM((span * blk * width, ncol), F32),
            pltpu.VMEM((span * unit, ncol), F32),
            pltpu.VMEM((span * unit, ncol), F32),
            pltpu.VMEM((span * unit, ncol), F32),
            pltpu.VMEM((span * unit, ncol), F32),
            pltpu.VMEM((npar, rows, ncol), F32),
            pltpu.VMEM((npar, rows + 2 * HALO, ncol), F32),
            pltpu.VMEM((-(-npar // 8) * 8, nimg), F32),
            pltpu.VMEM((-(-TAPS // 8) * 8, ncol), F32),
            pltpu.VMEM((kdim, nimg), F32),
            pltpu.VMEM((nimg, kdim), BF16),
            pltpu.VMEM((2 * width, nimg), BF16),
            pltpu.VMEM((2, blk * width, ncol), BF16),
            pltpu.VMEM((blk * width, ncol), BF16),
            pltpu.VMEM((blk * width, ncol), BF16),
            pltpu.VMEM((2 * half_rows, ncol), F32),
            pltpu.VMEM((half_rows, ncol), F32),
            pltpu.VMEM((2 * half_rows, ncol), F32),
            pltpu.VMEM((half_rows, ncol), F32),
            pltpu.VMEM((span * unit, ncol), BF16),
            pltpu.VMEM((2, 2 * unit, ncol), BF16),
            pltpu.VMEM((nrg * unit, ncol), BF16),
            pltpu.VMEM((2, edge, ncol), BF16),
            pltpu.VMEM((waves, span * unit, ncol), BF16),
            pltpu.VMEM((waves, 2 * unit, ncol), BF16),
            pltpu.VMEM((waves, 2 * unit, ncol), BF16),
            pltpu.VMEM((waves, nrg * unit, ncol), BF16),
            pltpu.VMEM((waves, edge, ncol), BF16),
            pltpu.VMEM((waves, edge, ncol), BF16),
            pltpu.VMEM((8, ncol), F32),
            pltpu.VMEM((8, ncol), F32),
            pltpu.VMEM((gsize * waves, 8, ncol), F32),
            pltpu.VMEM((ngroup, 8, ncol), F32),
            dma((4,)),
            dma((8,)), dma((8,)),
            dma((2, waves)), dma((2, waves)),
            dma((2, waves)), dma((2, waves)),
            dma((2, waves)), dma((2, waves)),
            dma((gsize * waves,)), dma((gsize * waves,)),
            dma((ngroup,)), dma((ngroup,)),
        ],
        compiler_params=pltpu.CompilerParams(
            collective_id=0, has_side_effects=True, vmem_limit_bytes=66_000_000
        ),
    )(
        params, dual_in, jacobian.reshape(images, rows, ncol),
        observed.reshape(nimg, rows, ncol), response, psf,
        step_size.reshape(1), dual_step.reshape(1), tv_bound.reshape(1), clip_bound.reshape(1),
    )
    state, dual_out, misfit = pl.pallas_call(
        hand_out,
        out_shape=(
            jax.ShapeDtypeStruct((npar, rows, ncol), F32),
            jax.ShapeDtypeStruct((2, npar, rows, ncol), F32),
            jax.ShapeDtypeStruct((1,), F32),
        ),
        in_specs=[vmem] * 3,
        out_specs=(hbm, hbm, smem),
        scratch_shapes=[dma((2,))],
        compiler_params=pltpu.CompilerParams(vmem_limit_bytes=1_000_000),
    )(state, dual_out, misfit)
    return state, dual_out, misfit.reshape(())


def solution(mesh):
    in_specs = (
        P(None, "tile", None),
        P(None, None, "tile", None),
        P(None, None, "tile", None),
        P(None, "wave"),
        P(None, "wave", "tile", None),
        P(),
        P(),
        P(),
        P(),
        P(),
    )
    out_specs = (P(None, "tile", None), P(None, None, "tile", None), P())
    return jax.shard_map(
        per_device, mesh=mesh, in_specs=in_specs, out_specs=out_specs, check_vma=False
    )
```

```python
import functools

import jax
import jax.numpy as jnp
from jax import lax
from jax.experimental import pallas as pl
from jax.experimental.pallas import tpu as pltpu
from jax.sharding import PartitionSpec as P

MESH = pl.DeviceIdType.MESH
HALO = 8
TAPS = 17
F32 = jnp.float32
BF16 = jnp.bfloat16


def split_hi_lo(value):
    high = value.astype(BF16).astype(F32)
    return high, value - high


def group_size(count):
    size = 1
    while size * size < count:
        size *= 2
    return size if count % size == 0 else count


def kernel(
    tiles, waves, total_count,
    params_h, dual_h, jac_h, obs_h, response_h, psf_h, step_h, dstep_h, bound_h, clip_h,
    x_out, d_out, m_out,
    response, psf, step_size, dual_step, tv_bound, clip_bound, params, dual, jac, obs,
    wt, main_a, half_a, obs_f, obs_l, jac_n, jac_l, x_l, lhs, tot, proj, prod, grad_c,
    x_c, div_c, base_c, div_n, dpad, respad, psfpad, rt, rbf, rtb,
    jac_up, jac_dn, par_up, par_dn, dual_up, jac_hn,
    full0, edge0, full1, edge1, full0_in, up0_in, dn0_in, full1_in, up1_in, dn1_in,
    m_own, m_mid, m_group, m_cross,
    local, in_send, in_recv, f_send, f_recv, u_send, u_recv, d_send, d_recv,
    mg_send, mg_recv, mc_send, mc_recv,
):
    npar, rows, ncol = params.shape
    images = jac.shape[0]
    stokes = images // npar
    nwave = response.shape[1]
    nimg = stokes * nwave
    width = -(-images // 8) * 8
    wide = -(-images // 16) * 16
    nrg = rows // HALO
    span = nrg + 2
    blk = HALO
    cols = ncol // blk
    unit = npar * blk
    me_t = lax.axis_index("tile")
    me_w = lax.axis_index("wave")
    up = lax.rem(me_t + tiles - 1, tiles)
    down = lax.rem(me_t + 1, tiles)
    gsize = group_size(tiles)
    ngroup = tiles // gsize
    my_group = me_t // gsize
    my_place = lax.rem(me_t, gsize)
    spin = [me_w] + [lax.rem(me_w + d, waves) for d in range(1, waves)]
    group_tiles = [me_t]
    group_tiles += [my_group * gsize + lax.rem(my_place + d, gsize) for d in range(1, gsize)]
    group_peers = [(t, w) for i, t in enumerate(group_tiles) for j, w in enumerate(spin) if i + j > 0]
    cross_peers = [
        (lax.rem(my_group + d, ngroup) * gsize + my_place, me_w) for d in range(1, ngroup)
    ]

    barrier = pltpu.get_barrier_semaphore()
    peers = [(up, me_w), (down, me_w)] + group_peers + cross_peers
    for peer in peers:
        pl.semaphore_signal(barrier, inc=1, device_id=peer, device_id_type=MESH)
    fetch = [
        pltpu.make_async_copy(jac_h, jac, local.at[0]),
        pltpu.make_async_copy(params_h, params, local.at[1]),
        pltpu.make_async_copy(dual_h, dual, local.at[2]),
        pltpu.make_async_copy(obs_h, obs, local.at[3]),
        pltpu.make_async_copy(psf_h, psf, local.at[4]),
        pltpu.make_async_copy(response_h, response, local.at[5]),
        pltpu.make_async_copy(step_h, step_size, local.at[6]),
        pltpu.make_async_copy(dstep_h, dual_step, local.at[7]),
        pltpu.make_async_copy(bound_h, tv_bound, local.at[8]),
        pltpu.make_async_copy(clip_h, clip_bound, local.at[9]),
    ]
    for copy in fetch:
        copy.start()

    lane = lax.broadcasted_iota(jnp.int32, (1, ncol), 1)
    group_bit = [(lane // (cols << b)) % 2 == 0 for b in range(3)]
    near = lane % cols < HALO

    def swap_blocks(parts):
        parts = list(parts)
        for b in range(3):
            k = 1 << b
            shift = cols * k
            for i in range(blk):
                if i & k:
                    continue
                one, two = parts[i], parts[i + k]
                parts[i] = jnp.where(group_bit[b], one, pltpu.roll(two, shift, 1))
                parts[i + k] = jnp.where(group_bit[b], pltpu.roll(one, ncol - shift, 1), two)
        return parts

    def image_rows(rg, b):
        return slice((rg * blk + b) * width, (rg * blk + b + 1) * width)

    def unit_rows(rg, b):
        return slice((rg * blk + b) * npar, (rg * blk + b + 1) * npar)

    def to_units(source, rg_from, target, rg_to):
        parts = swap_blocks([source[:, rg_from * HALO + r, :] for r in range(HALO)])
        for b in range(blk):
            target[unit_rows(rg_to, b), :] = parts[b]

    def to_blocks(source, height, rg_from, rg_to):
        for g in range(width // 8):
            at = g * 8 * height + rg_from * HALO
            parts = swap_blocks([source[pl.ds(at + r, 8, stride=height), :] for r in range(HALO)])
            for b in range(blk):
                at = (rg_to * blk + b) * width + g * 8
                jac_l[at:at + 8, :] = parts[b]

    def remote(src, dst, send, recv, peer):
        return pltpu.make_async_remote_copy(
            src_ref=src, dst_ref=dst, send_sem=send, recv_sem=recv,
            device_id=peer, device_id_type=MESH,
        )

    above, below = (up, me_w), (down, me_w)

    def unit_span(rg, count):
        return pl.ds(rg * unit, count * unit)

    top, last = pl.ds(0, HALO), pl.ds(rows - HALO, HALO)
    first = [
        remote(jac_h.at[:, last], jac_up, in_send.at[0], in_recv.at[0], below),
        remote(jac_h.at[:, top], jac_dn, in_send.at[1], in_recv.at[1], above),
        remote(params_h.at[:, last], par_up, in_send.at[2], in_recv.at[2], below),
        remote(params_h.at[:, top], par_dn, in_send.at[3], in_recv.at[3], above),
        remote(dual_h.at[0, :, last], dual_up, in_send.at[4], in_recv.at[4], below),
    ]
    fetch[4].wait()
    psfpad[...] = jnp.zeros_like(psfpad)
    psfpad[0:TAPS, 0:TAPS] = psf[...].astype(F32)
    taps = pltpu.roll(psfpad[...], ncol - HALO, 1)
    for tap in range(TAPS):
        line = jnp.broadcast_to(taps[tap:tap + 1, :], (cols, ncol))
        line = pltpu.roll(line, 0, 1, stride=1, stride_axis=0)
        side = jnp.where(near, pltpu.roll(line, ncol - cols, 1), pltpu.roll(line, cols, 1))
        for ref, value in ((main_a, line), (half_a, side)):
            value = jnp.where(lane < cols, value, 0.0)
            for b in range(3):
                value = value + pltpu.roll(value, cols << b, 1)
            ref[tap * cols:(tap + 1) * cols, :] = value
    wt[0, ncol:, :] = jnp.zeros((wt.shape[1] - ncol, 2 * ncol), BF16)
    for rg in range(1, span):
        for ro in range(nrg):
            if not 0 <= rg - ro <= 2:
                wt[rg, ro * ncol:(ro + 1) * ncol, :] = jnp.zeros((ncol, 2 * ncol), BF16)
    for delta in range(3):
        for r in range(HALO):
            for part, ref in ((0, main_a), (1, half_a)):
                value = jnp.zeros((cols, ncol), F32)
                for kr in range(HALO):
                    tap = delta * HALO + kr - r
                    if 0 <= tap < TAPS:
                        value = jnp.where(lane // cols == kr, ref[tap * cols:(tap + 1) * cols, :], value)
                value = value.astype(BF16)
                for ro in range(nrg):
                    at = ro * ncol + r * cols
                    wt[ro + delta, at:at + cols, part * ncol:(part + 1) * ncol] = value

    pl.semaphore_wait(barrier, len(peers))
    for copy in first:
        copy.start()

    jac_n[images * rows:, :] = jnp.zeros((jac_n.shape[0] - images * rows, ncol), F32)
    jac_hn[images * HALO:, :] = jnp.zeros((jac_hn.shape[0] - images * HALO, ncol), F32)
    edge1[...] = jnp.zeros_like(edge1)
    fetch[0].wait()
    for m in range(images):
        jac_n[m * rows:(m + 1) * rows, :] = jac[m].astype(F32)
    for rg in range(nrg):
        to_blocks(jac_n, rows, rg, rg + 1)
    fetch[1].wait()
    for rg in range(nrg):
        to_units(params, rg, x_c, rg + 1)
    for copy in fetch[5:]:
        copy.wait()

    step = step_size[0]
    clip = clip_bound[0]
    bound = tv_bound[0]
    dstep = dual_step[0]

    def expand(rg):
        for b in range(blk):
            value = x_c[unit_rows(rg, b), :]
            at = (rg * blk + b) * width
            for s in range(stokes):
                x_l[at + s * npar:at + (s + 1) * npar, :] = value

    def build(rg):
        terms = [jac_l[image_rows(rg, b), :] * x_l[image_rows(rg, b), :] for b in range(blk)]
        for b in range(blk):
            side = jnp.where(near, terms[(b + 1) % blk], terms[(b + blk - 1) % blk])
            at = (rg * blk + b) * 2 * width
            for part, value in ((0, terms[b]), (1, side)):
                value = jnp.concatenate(split_hi_lo(value), axis=0).astype(BF16)
                lhs[at:at + 2 * width, part * ncol:(part + 1) * ncol] = value

    def forward(rg):
        window = lhs[rg * blk * 2 * width:(rg + 1) * blk * 2 * width, :]
        return lax.dot_general(
            window, wt[rg], (((1,), (1,)), ((), ())), preferred_element_type=F32
        )

    if width > images:
        for rg in range(span):
            for b in range(blk):
                at = (rg * blk + b) * width
                x_l[at + images:at + width, :] = jnp.zeros((width - images, ncol), F32)
    for rg in range(1, nrg + 1):
        expand(rg)
        build(rg)
    own = None
    for rg in range(1, nrg + 1):
        part = forward(rg)
        own = part if own is None else own + part
    tot[...] = own

    respad[...] = jnp.zeros_like(respad)
    respad[0:npar, 0:nwave] = response[...]
    rt[...] = jnp.zeros_like(rt)
    spread = respad[...]
    for s in range(stokes):
        shifted = spread if s == 0 else pltpu.roll(spread, s * nwave, 1)
        for part in range(3):
            at = part * width + s * npar
            rt[at:at + npar, :] = shifted[0:npar]
    full = rt[...]
    high, low = split_hi_lo(full)
    place = lax.broadcasted_iota(jnp.int32, full.shape, 0)
    rbf[...] = jnp.where(place < 2 * width, high, low).T.astype(BF16)
    rtb[...] = jnp.concatenate([high[0:width], low[0:width]], axis=0).astype(BF16)

    fetch[3].wait()
    obs_f[...] = obs[...].astype(F32).reshape(nimg * rows, ncol)
    def turn(g, carry):
        for rg in range(nrg):
            source = pl.multiple_of(g * 8 * rows, 8 * rows) + rg * HALO
            parts = swap_blocks([obs_f[pl.ds(source + r, 8, stride=rows), :] for r in range(HALO)])
            for b in range(blk):
                at = pl.multiple_of(b * nimg + g * 8, 8)
                obs_l[pl.ds(at, 8), rg * ncol:(rg + 1) * ncol] = parts[b]
        return carry

    lax.fori_loop(0, nimg // 8, turn, 0, unroll=4)
    for copy in first[:4]:
        copy.wait()
    for source, rg in ((jac_up, 0), (jac_dn, nrg + 1)):
        for m in range(images):
            jac_hn[m * HALO:(m + 1) * HALO, :] = source[m].astype(F32)
        to_blocks(jac_hn, HALO, 0, rg)
    to_units(par_up, 0, x_c, 0)
    to_units(par_dn, 0, x_c, nrg + 1)
    zero_k = jnp.zeros((rbf.shape[1] - 3 * width, nrg * ncol), F32)

    def widen(value):
        if wide == width:
            return value.astype(BF16)
        fill = jnp.zeros((wide - width, value.shape[1]), F32)
        return jnp.concatenate([value, fill], axis=0).astype(BF16)

    for it in range(2):
        for rg in (0, nrg + 1) if it == 0 else range(span):
            expand(rg)
            build(rg)
        if it == 0:
            total = tot[...] + forward(0) + forward(nrg + 1)
        else:
            total = None
            for rg in range(span):
                part = forward(rg)
                total = part if total is None else total + part
        loss = jnp.zeros((8, nrg * ncol), F32)
        def respond(b):
            both = total[b * 2 * width:(b + 1) * 2 * width]
            bhi, blo = split_hi_lo(both[:width] + both[width:])
            stack = jnp.concatenate([bhi, blo, bhi, zero_k], axis=0).astype(BF16)
            return jnp.dot(rbf[...], stack, preferred_element_type=F32)

        coming = respond(0)
        for b in range(blk):
            blurred = coming
            if b + 1 < blk:
                coming = respond(b + 1)
            resid = blurred - obs_l[b * nimg:(b + 1) * nimg, :]
            held = jnp.clip(resid, -clip, clip)
            if it == 0:
                huber = held * (resid - 0.5 * held)
                loss = loss + jnp.sum(huber.reshape(nimg // 8, 8, nrg * ncol), axis=0)
            both = jnp.dot(rtb[...], held.astype(BF16), preferred_element_type=F32)
            proj[b * wide:(b + 1) * wide, :] = widen(both[:width] + both[width:])
        if it == 0:
            loss = sum(loss[:, i * ncol:(i + 1) * ncol] for i in range(nrg))
            m_own[...] = loss
            slot = my_place * waves + me_w
            m_group[slot] = loss
            copies_g = [
                remote(m_own, m_group.at[slot], mg_send.at[d], mg_recv.at[d], peer)
                for d, peer in enumerate(group_peers)
            ]
            for copy in copies_g:
                copy.start()
        for rg in range(span):
            back = jnp.dot(proj[...], wt[rg], preferred_element_type=F32)
            mains = [back[b * wide:b * wide + width, 0:ncol] for b in range(blk)]
            sides = [back[b * wide:b * wide + width, ncol:] for b in range(blk)]
            for b in range(blk):
                along = mains[b] + jnp.where(near, sides[(b + blk - 1) % blk], sides[(b + 1) % blk])
                at = (rg * blk + b) * width
                prod[at:at + width, :] = jac_l[at:at + width, :] * along
                grad = None
                for s in range(stokes):
                    part = prod[at + s * npar:at + (s + 1) * npar, :]
                    grad = part if grad is None else grad + part
                grad_c[unit_rows(rg, b), :] = grad
        reach = 2 * unit if it == 0 else unit
        size = span * unit
        start = 0 if it == 0 else unit
        full_out, edge_out = (full0, edge0) if it == 0 else (full1, edge1)
        full_in, up_in, dn_in = (full0_in, up0_in, dn0_in) if it == 0 else (full1_in, up1_in, dn1_in)
        edge_out[0, 0:reach, :] = grad_c[0:reach, :].astype(BF16)
        edge_out[1, 0:reach, :] = grad_c[size - reach:, :].astype(BF16)
        whole = grad_c[start:size - start, :].astype(BF16)
        full_out[...] = whole
        full_in[me_w] = whole
        copies = []
        for d in range(waves - 1, -1, -1):
            copies += [
                remote(edge_out.at[1], up_in.at[me_w], u_send.at[it, d], u_recv.at[it, d], (down, spin[d])),
                remote(edge_out.at[0], dn_in.at[me_w], d_send.at[it, d], d_recv.at[it, d], (up, spin[d])),
            ]
        for d in range(1, waves):
            copies.append(
                remote(full_out, full_in.at[me_w], f_send.at[it, d], f_recv.at[it, d], (me_t, spin[d]))
            )
        for copy in copies:
            copy.start()
        if it == 0:
            fetch[2].wait()
            first[4].wait()
            now = params[...]
            d1 = pltpu.roll(now, ncol - 1, 2) - now
            d1 = jnp.clip(dual[1] + dstep * d1, -bound, bound)
            d_out[1] = d1
            dpad[:, HALO:HALO + rows, :] = now
            dpad[:, HALO + rows, :] = par_dn[:, 0, :]
            d0 = dpad[:, HALO + 1:HALO + 1 + rows, :] - now
            d0 = jnp.clip(dual[0] + dstep * d0, -bound, bound)
            d_out[0] = d0
            side = params[:, 0, :] - par_up[:, HALO - 1, :]
            side = jnp.clip(dual_up[:, HALO - 1, :] + dstep * side, -bound, bound)
            dpad[:, HALO - 1, :] = side
            dpad[:, HALO:HALO + rows, :] = d0
            div_n[...] = (d0 - dpad[:, HALO - 1:HALO - 1 + rows, :]) + (d1 - pltpu.roll(d1, 1, 2))
            for rg in range(nrg):
                to_units(div_n, rg, div_c, rg + 1)
            copies_v = [
                remote(
                    div_c.at[unit_span(nrg, 1)], div_c.at[unit_span(0, 1)],
                    in_send.at[5], in_recv.at[5], below,
                ),
                remote(
                    div_c.at[unit_span(1, 1)], div_c.at[unit_span(nrg + 1, 1)],
                    in_send.at[6], in_recv.at[6], above,
                ),
            ]
            for copy in copies_v:
                copy.start()
            for copy in copies_v:
                copy.wait()
            base_c[...] = x_c[...] + step * div_c[...]
        else:
            base_c[unit:size - unit, :] = x_c[unit:size - unit, :] + step * div_c[unit:size - unit, :]
            for copy in copies_g:
                copy.wait()
            total_m = m_group[0]
            for g in range(1, gsize * waves):
                total_m = total_m + m_group[g]
            m_mid[...] = total_m
            m_cross[my_group] = total_m
            copies_c = [
                remote(m_mid, m_cross.at[my_group], mc_send.at[d], mc_recv.at[d], peer)
                for d, peer in enumerate(cross_peers)
            ]
            for copy in copies_c:
                copy.start()
            for copy in copies_c:
                copy.wait()
            tot_m = m_cross[0]
            for g in range(1, ngroup):
                tot_m = tot_m + m_cross[g]
            m_out[...] = jnp.full((8, ncol), jnp.sum(tot_m) / total_count, F32)
        for copy in copies:
            copy.wait()

        def added(ref, count):
            value = ref[0, 0:count, :].astype(F32)
            for w in range(1, waves):
                value = value + ref[w, 0:count, :].astype(F32)
            return value

        inner = added(full_in, size - 2 * start)
        top = inner[:reach] + added(up_in, reach)
        low = inner[size - 2 * start - reach:] + added(dn_in, reach)
        end = size - start
        x_c[start:start + reach, :] = base_c[start:start + reach, :] - step * top
        if end - start > 2 * reach:
            x_c[start + reach:end - reach, :] = (
                base_c[start + reach:end - reach, :] - step * inner[reach:end - start - reach]
            )
        x_c[end - reach:end, :] = base_c[end - reach:end, :] - step * low
    for rg in range(nrg):
        parts = swap_blocks([x_c[unit_rows(rg + 1, b), :] for b in range(blk)])
        for r in range(HALO):
            x_out[:, rg * HALO + r, :] = parts[r]


def hand_out(x, d, m, x_h, d_h, m_h, m_s, sem):
    copies = [pltpu.make_async_copy(x, x_h, sem.at[0]), pltpu.make_async_copy(d, d_h, sem.at[1])]
    for copy in copies:
        copy.start()
    m_s[0] = m[0, 0]
    copies.append(pltpu.make_async_copy(m_s, m_h, sem.at[2]))
    copies[2].start()
    for copy in copies:
        copy.wait()


def per_device(
    params, dual_in, jacobian, response, observed, psf, step_size, dual_step, tv_bound, clip_bound
):
    stokes, nwave, rows, ncol = observed.shape
    npar = params.shape[0]
    nimg = stokes * nwave
    images = stokes * npar
    width = -(-images // 8) * 8
    wide = -(-images // 16) * 16
    kdim = -(-3 * width // 128) * 128
    nrg = rows // HALO
    span = nrg + 2
    blk = HALO
    cols = ncol // blk
    unit = npar * blk
    edge = -(-unit // 16) * 16
    tiles = lax.axis_size("tile")
    waves = lax.axis_size("wave")
    total_count = float(nimg * waves * rows * tiles * ncol)
    gsize = group_size(tiles)
    ngroup = tiles // gsize
    vmem = pl.BlockSpec(memory_space=pltpu.VMEM)
    smem = pl.BlockSpec(memory_space=pltpu.SMEM)
    hbm = pl.BlockSpec(memory_space=pltpu.HBM)
    dma = pltpu.SemaphoreType.DMA
    state, dual_out, misfit = pl.pallas_call(
        functools.partial(kernel, tiles, waves, total_count),
        out_shape=(
            pltpu.VMEM((npar, rows, ncol), F32),
            pltpu.VMEM((2, npar, rows, ncol), F32),
            pltpu.VMEM((8, ncol), F32),
        ),
        in_specs=[hbm] * 10,
        out_specs=(vmem, vmem, vmem),
        scratch_shapes=[
            pltpu.VMEM(response.shape, F32),
            pltpu.VMEM(psf.shape, BF16),
            pltpu.SMEM((1,), F32),
            pltpu.SMEM((1,), F32),
            pltpu.SMEM((1,), F32),
            pltpu.SMEM((1,), F32),
            pltpu.VMEM((npar, rows, ncol), F32),
            pltpu.VMEM((2, npar, rows, ncol), F32),
            pltpu.VMEM((images, rows, ncol), BF16),
            pltpu.VMEM((nimg, rows, ncol), BF16),
            pltpu.VMEM((span, nrg * ncol, 2 * ncol), BF16),
            pltpu.VMEM((TAPS * cols, ncol), F32),
            pltpu.VMEM((TAPS * cols, ncol), F32),
            pltpu.VMEM((nimg * rows, ncol), F32),
            pltpu.VMEM((blk * nimg, nrg * ncol), F32),
            pltpu.VMEM((width * rows, ncol), F32),
            pltpu.VMEM((span * blk * width, ncol), F32),
            pltpu.VMEM((span * blk * width, ncol), F32),
            pltpu.VMEM((span * blk * 2 * width, 2 * ncol), BF16),
            pltpu.VMEM((blk * 2 * width, nrg * ncol), F32),
            pltpu.VMEM((blk * wide, nrg * ncol), BF16),
            pltpu.VMEM((span * blk * width, ncol), F32),
            pltpu.VMEM((span * unit, ncol), F32),
            pltpu.VMEM((span * unit, ncol), F32),
            pltpu.VMEM((span * unit, ncol), F32),
            pltpu.VMEM((span * unit, ncol), F32),
            pltpu.VMEM((npar, rows, ncol), F32),
            pltpu.VMEM((npar, rows + 2 * HALO, ncol), F32),
            pltpu.VMEM((-(-npar // 8) * 8, nimg), F32),
            pltpu.VMEM((-(-TAPS // 8) * 8, ncol), F32),
            pltpu.VMEM((kdim, nimg), F32),
            pltpu.VMEM((nimg, kdim), BF16),
            pltpu.VMEM((2 * width, nimg), BF16),
            pltpu.VMEM((images, HALO, ncol), BF16),
            pltpu.VMEM((images, HALO, ncol), BF16),
            pltpu.VMEM((npar, HALO, ncol), F32),
            pltpu.VMEM((npar, HALO, ncol), F32),
            pltpu.VMEM((npar, HALO, ncol), F32),
            pltpu.VMEM((width * HALO, ncol), F32),
            pltpu.VMEM((span * unit, ncol), BF16),
            pltpu.VMEM((2, 2 * unit, ncol), BF16),
            pltpu.VMEM((nrg * unit, ncol), BF16),
            pltpu.VMEM((2, edge, ncol), BF16),
            pltpu.VMEM((waves, span * unit, ncol), BF16),
            pltpu.VMEM((waves, 2 * unit, ncol), BF16),
            pltpu.VMEM((waves, 2 * unit, ncol), BF16),
            pltpu.VMEM((waves, nrg * unit, ncol), BF16),
            pltpu.VMEM((waves, edge, ncol), BF16),
            pltpu.VMEM((waves, edge, ncol), BF16),
            pltpu.VMEM((8, ncol), F32),
            pltpu.VMEM((8, ncol), F32),
            pltpu.VMEM((gsize * waves, 8, ncol), F32),
            pltpu.VMEM((ngroup, 8, ncol), F32),
            dma((10,)),
            dma((7,)), dma((7,)),
            dma((2, waves)), dma((2, waves)),
            dma((2, waves)), dma((2, waves)),
            dma((2, waves)), dma((2, waves)),
            dma((gsize * waves,)), dma((gsize * waves,)),
            dma((ngroup,)), dma((ngroup,)),
        ],
        compiler_params=pltpu.CompilerParams(
            collective_id=0, has_side_effects=True, vmem_limit_bytes=66_000_000
        ),
    )(
        params, dual_in, jacobian.reshape(images, rows, ncol),
        observed.reshape(nimg, rows, ncol), response, psf,
        step_size.reshape(1), dual_step.reshape(1), tv_bound.reshape(1), clip_bound.reshape(1),
    )
    state, dual_out, misfit = pl.pallas_call(
        hand_out,
        out_shape=(
            jax.ShapeDtypeStruct((npar, rows, ncol), F32),
            jax.ShapeDtypeStruct((2, npar, rows, ncol), F32),
            jax.ShapeDtypeStruct((1,), F32),
        ),
        in_specs=[vmem] * 3,
        out_specs=(hbm, hbm, hbm),
        scratch_shapes=[pltpu.SMEM((1,), F32), dma((3,))],
        compiler_params=pltpu.CompilerParams(vmem_limit_bytes=1_000_000),
    )(state, dual_out, misfit)
    return state, dual_out, misfit.reshape(())


def solution(mesh):
    in_specs = (
        P(None, "tile", None),
        P(None, None, "tile", None),
        P(None, None, "tile", None),
        P(None, "wave"),
        P(None, "wave", "tile", None),
        P(),
        P(),
        P(),
        P(),
        P(),
    )
    out_specs = (P(None, "tile", None), P(None, None, "tile", None), P())
    return jax.shard_map(
        per_device, mesh=mesh, in_specs=in_specs, out_specs=out_specs, check_vma=False
    )
```

```python
import functools

import jax
import jax.numpy as jnp
from jax import lax
from jax.experimental import pallas as pl
from jax.experimental.pallas import tpu as pltpu
from jax.sharding import PartitionSpec as P

MESH = pl.DeviceIdType.MESH
HALO = 8
TAPS = 17
F32 = jnp.float32
BF16 = jnp.bfloat16


def split_hi_lo(value):
    high = value.astype(BF16).astype(F32)
    return high, value - high


def group_size(count):
    size = 1
    while size * size < count:
        size *= 2
    return size if count % size == 0 else count


def kernel(
    tiles, waves, total_count,
    params_h, dual_h, jac_h, obs_h, response_h, psf_h, step_h, dstep_h, bound_h, clip_h,
    x_out, d_out, m_out,
    response, psf, step_size, dual_step, tv_bound, clip_bound, params, dual, jac, obs,
    wt, main_a, half_a, obs_f, obs_l, jac_n, jac_l, x_l, lhs, tot, proj, prod, grad_c,
    x_c, div_c, base_c, div_n, dpad, respad, psfpad, rt, rbf, rtb,
    jac_up, jac_dn, par_up, par_dn, dual_up, jac_hn,
    full0, edge0, full1, edge1, full0_in, up0_in, dn0_in, full1_in, up1_in, dn1_in,
    m_own, m_mid, m_group, m_cross,
    local, in_send, in_recv, f_send, f_recv, u_send, u_recv, d_send, d_recv,
    mg_send, mg_recv, mc_send, mc_recv,
):
    npar, rows, ncol = params.shape
    images = jac.shape[0]
    stokes = images // npar
    nwave = response.shape[1]
    nimg = stokes * nwave
    width = -(-images // 8) * 8
    nrg = rows // HALO
    span = nrg + 2
    blk = HALO
    cols = ncol // blk
    unit = npar * blk
    me_t = lax.axis_index("tile")
    me_w = lax.axis_index("wave")
    up = lax.rem(me_t + tiles - 1, tiles)
    down = lax.rem(me_t + 1, tiles)
    gsize = group_size(tiles)
    ngroup = tiles // gsize
    my_group = me_t // gsize
    my_place = lax.rem(me_t, gsize)
    spin = [me_w] + [lax.rem(me_w + d, waves) for d in range(1, waves)]
    group_tiles = [me_t]
    group_tiles += [my_group * gsize + lax.rem(my_place + d, gsize) for d in range(1, gsize)]
    group_peers = [(t, w) for i, t in enumerate(group_tiles) for j, w in enumerate(spin) if i + j > 0]
    cross_peers = [
        (lax.rem(my_group + d, ngroup) * gsize + my_place, me_w) for d in range(1, ngroup)
    ]

    barrier = pltpu.get_barrier_semaphore()
    peers = [(up, me_w), (down, me_w)] + group_peers + cross_peers
    for peer in peers:
        pl.semaphore_signal(barrier, inc=1, device_id=peer, device_id_type=MESH)
    fetch = [
        pltpu.make_async_copy(jac_h, jac, local.at[0]),
        pltpu.make_async_copy(params_h, params, local.at[1]),
        pltpu.make_async_copy(dual_h, dual, local.at[2]),
        pltpu.make_async_copy(obs_h, obs, local.at[3]),
        pltpu.make_async_copy(psf_h, psf, local.at[4]),
        pltpu.make_async_copy(response_h, response, local.at[5]),
        pltpu.make_async_copy(step_h, step_size, local.at[6]),
        pltpu.make_async_copy(dstep_h, dual_step, local.at[7]),
        pltpu.make_async_copy(bound_h, tv_bound, local.at[8]),
        pltpu.make_async_copy(clip_h, clip_bound, local.at[9]),
    ]
    for copy in fetch:
        copy.start()

    lane = lax.broadcasted_iota(jnp.int32, (1, ncol), 1)
    group_bit = [(lane // (cols << b)) % 2 == 0 for b in range(3)]
    near = lane % cols < HALO

    def swap_blocks(parts):
        parts = list(parts)
        for b in range(3):
            k = 1 << b
            shift = cols * k
            for i in range(blk):
                if i & k:
                    continue
                one, two = parts[i], parts[i + k]
                parts[i] = jnp.where(group_bit[b], one, pltpu.roll(two, shift, 1))
                parts[i + k] = jnp.where(group_bit[b], pltpu.roll(one, ncol - shift, 1), two)
        return parts

    def image_rows(rg, b):
        return slice((rg * blk + b) * width, (rg * blk + b + 1) * width)

    def unit_rows(rg, b):
        return slice((rg * blk + b) * npar, (rg * blk + b + 1) * npar)

    def to_units(source, rg_from, target, rg_to):
        parts = swap_blocks([source[:, rg_from * HALO + r, :] for r in range(HALO)])
        for b in range(blk):
            target[unit_rows(rg_to, b), :] = parts[b]

    def to_blocks(source, height, rg_from, rg_to):
        for g in range(width // 8):
            at = g * 8 * height + rg_from * HALO
            parts = swap_blocks([source[pl.ds(at + r, 8, stride=height), :] for r in range(HALO)])
            for b in range(blk):
                at = (rg_to * blk + b) * width + g * 8
                jac_l[at:at + 8, :] = parts[b]

    def remote(src, dst, send, recv, peer):
        return pltpu.make_async_remote_copy(
            src_ref=src, dst_ref=dst, send_sem=send, recv_sem=recv,
            device_id=peer, device_id_type=MESH,
        )

    above, below = (up, me_w), (down, me_w)

    def unit_span(rg, count):
        return pl.ds(rg * unit, count * unit)

    top, last = pl.ds(0, HALO), pl.ds(rows - HALO, HALO)
    first = [
        remote(jac_h.at[:, last], jac_up, in_send.at[0], in_recv.at[0], below),
        remote(jac_h.at[:, top], jac_dn, in_send.at[1], in_recv.at[1], above),
        remote(params_h.at[:, last], par_up, in_send.at[2], in_recv.at[2], below),
        remote(params_h.at[:, top], par_dn, in_send.at[3], in_recv.at[3], above),
        remote(dual_h.at[0, :, last], dual_up, in_send.at[4], in_recv.at[4], below),
    ]
    fetch[4].wait()
    psfpad[...] = jnp.zeros_like(psfpad)
    psfpad[0:TAPS, 0:TAPS] = psf[...].astype(F32)
    taps = pltpu.roll(psfpad[...], ncol - HALO, 1)
    for tap in range(TAPS):
        line = jnp.broadcast_to(taps[tap:tap + 1, :], (cols, ncol))
        line = pltpu.roll(line, 0, 1, stride=1, stride_axis=0)
        side = jnp.where(near, pltpu.roll(line, ncol - cols, 1), pltpu.roll(line, cols, 1))
        for ref, value in ((main_a, line), (half_a, side)):
            value = jnp.where(lane < cols, value, 0.0)
            for b in range(3):
                value = value + pltpu.roll(value, cols << b, 1)
            ref[tap * cols:(tap + 1) * cols, :] = value
    wt[0, ncol:, :] = jnp.zeros((wt.shape[1] - ncol, 2 * ncol), BF16)
    for rg in range(1, span):
        for ro in range(nrg):
            if not 0 <= rg - ro <= 2:
                wt[rg, ro * ncol:(ro + 1) * ncol, :] = jnp.zeros((ncol, 2 * ncol), BF16)
    for delta in range(3):
        for r in range(HALO):
            for part, ref in ((0, main_a), (1, half_a)):
                value = jnp.zeros((cols, ncol), F32)
                for kr in range(HALO):
                    tap = delta * HALO + kr - r
                    if 0 <= tap < TAPS:
                        value = jnp.where(lane // cols == kr, ref[tap * cols:(tap + 1) * cols, :], value)
                value = value.astype(BF16)
                for ro in range(nrg):
                    at = ro * ncol + r * cols
                    wt[ro + delta, at:at + cols, part * ncol:(part + 1) * ncol] = value

    pl.semaphore_wait(barrier, len(peers))
    for copy in first:
        copy.start()

    jac_n[images * rows:, :] = jnp.zeros((jac_n.shape[0] - images * rows, ncol), F32)
    jac_hn[images * HALO:, :] = jnp.zeros((jac_hn.shape[0] - images * HALO, ncol), F32)
    edge1[...] = jnp.zeros_like(edge1)
    fetch[0].wait()
    for m in range(images):
        jac_n[m * rows:(m + 1) * rows, :] = jac[m].astype(F32)
    for rg in range(nrg):
        to_blocks(jac_n, rows, rg, rg + 1)
    fetch[1].wait()
    for rg in range(nrg):
        to_units(params, rg, x_c, rg + 1)
    for copy in fetch[5:]:
        copy.wait()

    step = step_size[0]
    clip = clip_bound[0]
    bound = tv_bound[0]
    dstep = dual_step[0]

    def expand(rg):
        for b in range(blk):
            value = x_c[unit_rows(rg, b), :]
            at = (rg * blk + b) * width
            for s in range(stokes):
                x_l[at + s * npar:at + (s + 1) * npar, :] = value

    def build(rg):
        terms = [jac_l[image_rows(rg, b), :] * x_l[image_rows(rg, b), :] for b in range(blk)]
        for b in range(blk):
            side = jnp.where(near, terms[(b + 1) % blk], terms[(b + blk - 1) % blk])
            at = (rg * blk + b) * 2 * width
            for part, value in ((0, terms[b]), (1, side)):
                value = jnp.concatenate(split_hi_lo(value), axis=0).astype(BF16)
                lhs[at:at + 2 * width, part * ncol:(part + 1) * ncol] = value

    def forward(rg):
        window = lhs[rg * blk * 2 * width:(rg + 1) * blk * 2 * width, :]
        return lax.dot_general(
            window, wt[rg], (((1,), (1,)), ((), ())), preferred_element_type=F32
        )

    if width > images:
        for rg in range(span):
            for b in range(blk):
                at = (rg * blk + b) * width
                x_l[at + images:at + width, :] = jnp.zeros((width - images, ncol), F32)
    for rg in range(1, nrg + 1):
        expand(rg)
        build(rg)
    own = None
    for rg in range(1, nrg + 1):
        part = forward(rg)
        own = part if own is None else own + part
    tot[...] = own

    respad[...] = jnp.zeros_like(respad)
    respad[0:npar, 0:nwave] = response[...]
    rt[...] = jnp.zeros_like(rt)
    spread = respad[...]
    for s in range(stokes):
        shifted = spread if s == 0 else pltpu.roll(spread, s * nwave, 1)
        for part in range(3):
            at = part * width + s * npar
            rt[at:at + npar, :] = shifted[0:npar]
    full = rt[...]
    high, low = split_hi_lo(full)
    place = lax.broadcasted_iota(jnp.int32, full.shape, 0)
    rbf[...] = jnp.where(place < 2 * width, high, low).T.astype(BF16)
    rtb[...] = jnp.concatenate([high[0:width], low[0:width]], axis=0).astype(BF16)

    fetch[3].wait()
    obs_f[...] = obs[...].astype(F32).reshape(nimg * rows, ncol)
    def turn(g, carry):
        for rg in range(nrg):
            source = pl.multiple_of(g * 8 * rows, 8 * rows) + rg * HALO
            parts = swap_blocks([obs_f[pl.ds(source + r, 8, stride=rows), :] for r in range(HALO)])
            for b in range(blk):
                at = pl.multiple_of(b * nimg + g * 8, 8)
                obs_l[pl.ds(at, 8), rg * ncol:(rg + 1) * ncol] = parts[b]
        return carry

    lax.fori_loop(0, nimg // 8, turn, 0, unroll=4)
    for copy in first[:4]:
        copy.wait()
    for source, rg in ((jac_up, 0), (jac_dn, nrg + 1)):
        for m in range(images):
            jac_hn[m * HALO:(m + 1) * HALO, :] = source[m].astype(F32)
        to_blocks(jac_hn, HALO, 0, rg)
    to_units(par_up, 0, x_c, 0)
    to_units(par_dn, 0, x_c, nrg + 1)
    zero_k = jnp.zeros((rbf.shape[1] - 3 * width, nrg * ncol), F32)

    for it in range(2):
        for rg in (0, nrg + 1) if it == 0 else range(span):
            expand(rg)
            build(rg)
        if it == 0:
            total = tot[...] + forward(0) + forward(nrg + 1)
        else:
            total = None
            for rg in range(span):
                part = forward(rg)
                total = part if total is None else total + part
        loss = jnp.zeros((8, nrg * ncol), F32)
        def respond(b):
            both = total[b * 2 * width:(b + 1) * 2 * width]
            bhi, blo = split_hi_lo(both[:width] + both[width:])
            stack = jnp.concatenate([bhi, blo, bhi, zero_k], axis=0).astype(BF16)
            return jnp.dot(rbf[...], stack, preferred_element_type=F32)

        def collect(b, held, before):
            both = jnp.dot(rtb[...], held, preferred_element_type=F32)
            both = both[:width] + both[width:]
            if b % 2 == 1:
                pair = jnp.concatenate([before, both], axis=0).astype(BF16)
                proj[(b - 1) * width:(b + 1) * width, :] = pair
            return both

        ahead = [respond(b) for b in range(4)]
        held_last = before = None
        for b in range(blk):
            if b + 4 < blk:
                ahead.append(respond(b + 4))
            blurred = ahead.pop(0)
            resid = blurred - obs_l[b * nimg:(b + 1) * nimg, :]
            held = jnp.clip(resid, -clip, clip)
            if it == 0:
                huber = held * (resid - 0.5 * held)
                loss = loss + jnp.sum(huber.reshape(nimg // 8, 8, nrg * ncol), axis=0)
            if b > 0:
                before = collect(b - 1, held_last, before)
            held_last = held.astype(BF16)
        collect(blk - 1, held_last, before)
        if it == 0:
            loss = sum(loss[:, i * ncol:(i + 1) * ncol] for i in range(nrg))
            m_own[...] = loss
            slot = my_place * waves + me_w
            m_group[slot] = loss
            copies_g = [
                remote(m_own, m_group.at[slot], mg_send.at[d], mg_recv.at[d], peer)
                for d, peer in enumerate(group_peers)
            ]
            for copy in copies_g:
                copy.start()
        for rg in range(span):
            used = slice(max(rg - 2, 0) * ncol, min(rg + 1, nrg) * ncol)
            back = jnp.dot(proj[:, used], wt[rg, used, :], preferred_element_type=F32)
            mains = [back[b * width:(b + 1) * width, 0:ncol] for b in range(blk)]
            sides = [back[b * width:(b + 1) * width, ncol:] for b in range(blk)]
            for b in range(blk):
                along = mains[b] + jnp.where(near, sides[(b + blk - 1) % blk], sides[(b + 1) % blk])
                at = (rg * blk + b) * width
                prod[at:at + width, :] = jac_l[at:at + width, :] * along
                grad = None
                for s in range(stokes):
                    part = prod[at + s * npar:at + (s + 1) * npar, :]
                    grad = part if grad is None else grad + part
                grad_c[unit_rows(rg, b), :] = grad
        reach = 2 * unit if it == 0 else unit
        size = span * unit
        start = 0 if it == 0 else unit
        full_out, edge_out = (full0, edge0) if it == 0 else (full1, edge1)
        full_in, up_in, dn_in = (full0_in, up0_in, dn0_in) if it == 0 else (full1_in, up1_in, dn1_in)
        edge_out[0, 0:reach, :] = grad_c[0:reach, :].astype(BF16)
        edge_out[1, 0:reach, :] = grad_c[size - reach:, :].astype(BF16)
        whole = grad_c[start:size - start, :].astype(BF16)
        full_out[...] = whole
        full_in[me_w] = whole
        copies = []
        for d in range(waves - 1, -1, -1):
            copies += [
                remote(edge_out.at[1], up_in.at[me_w], u_send.at[it, d], u_recv.at[it, d], (down, spin[d])),
                remote(edge_out.at[0], dn_in.at[me_w], d_send.at[it, d], d_recv.at[it, d], (up, spin[d])),
            ]
        for d in range(1, waves):
            copies.append(
                remote(full_out, full_in.at[me_w], f_send.at[it, d], f_recv.at[it, d], (me_t, spin[d]))
            )
        for copy in copies:
            copy.start()
        if it == 0:
            fetch[2].wait()
            first[4].wait()
            now = params[...]
            d1 = pltpu.roll(now, ncol - 1, 2) - now
            d1 = jnp.clip(dual[1] + dstep * d1, -bound, bound)
            d_out[1] = d1
            dpad[:, HALO:HALO + rows, :] = now
            dpad[:, HALO + rows, :] = par_dn[:, 0, :]
            d0 = dpad[:, HALO + 1:HALO + 1 + rows, :] - now
            d0 = jnp.clip(dual[0] + dstep * d0, -bound, bound)
            d_out[0] = d0
            side = params[:, 0, :] - par_up[:, HALO - 1, :]
            side = jnp.clip(dual_up[:, HALO - 1, :] + dstep * side, -bound, bound)
            dpad[:, HALO - 1, :] = side
            dpad[:, HALO:HALO + rows, :] = d0
            div_n[...] = (d0 - dpad[:, HALO - 1:HALO - 1 + rows, :]) + (d1 - pltpu.roll(d1, 1, 2))
            for rg in range(nrg):
                to_units(div_n, rg, div_c, rg + 1)
            copies_v = [
                remote(
                    div_c.at[unit_span(nrg, 1)], div_c.at[unit_span(0, 1)],
                    in_send.at[5], in_recv.at[5], below,
                ),
                remote(
                    div_c.at[unit_span(1, 1)], div_c.at[unit_span(nrg + 1, 1)],
                    in_send.at[6], in_recv.at[6], above,
                ),
            ]
            for copy in copies_v:
                copy.start()
            for copy in copies_v:
                copy.wait()
            base_c[...] = x_c[...] + step * div_c[...]
        else:
            base_c[unit:size - unit, :] = x_c[unit:size - unit, :] + step * div_c[unit:size - unit, :]
            for copy in copies_g:
                copy.wait()
            total_m = m_group[0]
            for g in range(1, gsize * waves):
                total_m = total_m + m_group[g]
            m_mid[...] = total_m
            m_cross[my_group] = total_m
            copies_c = [
                remote(m_mid, m_cross.at[my_group], mc_send.at[d], mc_recv.at[d], peer)
                for d, peer in enumerate(cross_peers)
            ]
            for copy in copies_c:
                copy.start()
            for copy in copies_c:
                copy.wait()
            tot_m = m_cross[0]
            for g in range(1, ngroup):
                tot_m = tot_m + m_cross[g]
            m_out[...] = jnp.full((8, ncol), jnp.sum(tot_m) / total_count, F32)
        for copy in copies:
            copy.wait()

        def added(ref, count):
            value = ref[0, 0:count, :].astype(F32)
            for w in range(1, waves):
                value = value + ref[w, 0:count, :].astype(F32)
            return value

        inner = added(full_in, size - 2 * start)
        top = inner[:reach] + added(up_in, reach)
        low = inner[size - 2 * start - reach:] + added(dn_in, reach)
        end = size - start
        x_c[start:start + reach, :] = base_c[start:start + reach, :] - step * top
        if end - start > 2 * reach:
            x_c[start + reach:end - reach, :] = (
                base_c[start + reach:end - reach, :] - step * inner[reach:end - start - reach]
            )
        x_c[end - reach:end, :] = base_c[end - reach:end, :] - step * low
    for rg in range(nrg):
        parts = swap_blocks([x_c[unit_rows(rg + 1, b), :] for b in range(blk)])
        for r in range(HALO):
            x_out[:, rg * HALO + r, :] = parts[r]


def hand_out(x, d, m, x_h, d_h, m_h, m_s, sem):
    copies = [pltpu.make_async_copy(x, x_h, sem.at[0]), pltpu.make_async_copy(d, d_h, sem.at[1])]
    for copy in copies:
        copy.start()
    m_s[0] = m[0, 0]
    copies.append(pltpu.make_async_copy(m_s, m_h, sem.at[2]))
    copies[2].start()
    for copy in copies:
        copy.wait()


def per_device(
    params, dual_in, jacobian, response, observed, psf, step_size, dual_step, tv_bound, clip_bound
):
    stokes, nwave, rows, ncol = observed.shape
    npar = params.shape[0]
    nimg = stokes * nwave
    images = stokes * npar
    width = -(-images // 8) * 8
    kdim = -(-3 * width // 128) * 128
    nrg = rows // HALO
    span = nrg + 2
    blk = HALO
    cols = ncol // blk
    unit = npar * blk
    edge = -(-unit // 16) * 16
    tiles = lax.axis_size("tile")
    waves = lax.axis_size("wave")
    total_count = float(nimg * waves * rows * tiles * ncol)
    gsize = group_size(tiles)
    ngroup = tiles // gsize
    vmem = pl.BlockSpec(memory_space=pltpu.VMEM)
    smem = pl.BlockSpec(memory_space=pltpu.SMEM)
    hbm = pl.BlockSpec(memory_space=pltpu.HBM)
    dma = pltpu.SemaphoreType.DMA
    state, dual_out, misfit = pl.pallas_call(
        functools.partial(kernel, tiles, waves, total_count),
        out_shape=(
            pltpu.VMEM((npar, rows, ncol), F32),
            pltpu.VMEM((2, npar, rows, ncol), F32),
            pltpu.VMEM((8, ncol), F32),
        ),
        in_specs=[hbm] * 10,
        out_specs=(vmem, vmem, vmem),
        scratch_shapes=[
            pltpu.VMEM(response.shape, F32),
            pltpu.VMEM(psf.shape, BF16),
            pltpu.SMEM((1,), F32),
            pltpu.SMEM((1,), F32),
            pltpu.SMEM((1,), F32),
            pltpu.SMEM((1,), F32),
            pltpu.VMEM((npar, rows, ncol), F32),
            pltpu.VMEM((2, npar, rows, ncol), F32),
            pltpu.VMEM((images, rows, ncol), BF16),
            pltpu.VMEM((nimg, rows, ncol), BF16),
            pltpu.VMEM((span, nrg * ncol, 2 * ncol), BF16),
            pltpu.VMEM((TAPS * cols, ncol), F32),
            pltpu.VMEM((TAPS * cols, ncol), F32),
            pltpu.VMEM((nimg * rows, ncol), F32),
            pltpu.VMEM((blk * nimg, nrg * ncol), F32),
            pltpu.VMEM((width * rows, ncol), F32),
            pltpu.VMEM((span * blk * width, ncol), F32),
            pltpu.VMEM((span * blk * width, ncol), F32),
            pltpu.VMEM((span * blk * 2 * width, 2 * ncol), BF16),
            pltpu.VMEM((blk * 2 * width, nrg * ncol), F32),
            pltpu.VMEM((blk * width, nrg * ncol), BF16),
            pltpu.VMEM((span * blk * width, ncol), F32),
            pltpu.VMEM((span * unit, ncol), F32),
            pltpu.VMEM((span * unit, ncol), F32),
            pltpu.VMEM((span * unit, ncol), F32),
            pltpu.VMEM((span * unit, ncol), F32),
            pltpu.VMEM((npar, rows, ncol), F32),
            pltpu.VMEM((npar, rows + 2 * HALO, ncol), F32),
            pltpu.VMEM((-(-npar // 8) * 8, nimg), F32),
            pltpu.VMEM((-(-TAPS // 8) * 8, ncol), F32),
            pltpu.VMEM((kdim, nimg), F32),
            pltpu.VMEM((nimg, kdim), BF16),
            pltpu.VMEM((2 * width, nimg), BF16),
            pltpu.VMEM((images, HALO, ncol), BF16),
            pltpu.VMEM((images, HALO, ncol), BF16),
            pltpu.VMEM((npar, HALO, ncol), F32),
            pltpu.VMEM((npar, HALO, ncol), F32),
            pltpu.VMEM((npar, HALO, ncol), F32),
            pltpu.VMEM((width * HALO, ncol), F32),
            pltpu.VMEM((span * unit, ncol), BF16),
            pltpu.VMEM((2, 2 * unit, ncol), BF16),
            pltpu.VMEM((nrg * unit, ncol), BF16),
            pltpu.VMEM((2, edge, ncol), BF16),
            pltpu.VMEM((waves, span * unit, ncol), BF16),
            pltpu.VMEM((waves, 2 * unit, ncol), BF16),
            pltpu.VMEM((waves, 2 * unit, ncol), BF16),
            pltpu.VMEM((waves, nrg * unit, ncol), BF16),
            pltpu.VMEM((waves, edge, ncol), BF16),
            pltpu.VMEM((waves, edge, ncol), BF16),
            pltpu.VMEM((8, ncol), F32),
            pltpu.VMEM((8, ncol), F32),
            pltpu.VMEM((gsize * waves, 8, ncol), F32),
            pltpu.VMEM((ngroup, 8, ncol), F32),
            dma((10,)),
            dma((7,)), dma((7,)),
            dma((2, waves)), dma((2, waves)),
            dma((2, waves)), dma((2, waves)),
            dma((2, waves)), dma((2, waves)),
            dma((gsize * waves,)), dma((gsize * waves,)),
            dma((ngroup,)), dma((ngroup,)),
        ],
        compiler_params=pltpu.CompilerParams(
            collective_id=0, has_side_effects=True, vmem_limit_bytes=66_000_000
        ),
    )(
        params, dual_in, jacobian.reshape(images, rows, ncol),
        observed.reshape(nimg, rows, ncol), response, psf,
        step_size.reshape(1), dual_step.reshape(1), tv_bound.reshape(1), clip_bound.reshape(1),
    )
    state, dual_out, misfit = pl.pallas_call(
        hand_out,
        out_shape=(
            jax.ShapeDtypeStruct((npar, rows, ncol), F32),
            jax.ShapeDtypeStruct((2, npar, rows, ncol), F32),
            jax.ShapeDtypeStruct((1,), F32),
        ),
        in_specs=[vmem] * 3,
        out_specs=(hbm, hbm, hbm),
        scratch_shapes=[pltpu.SMEM((1,), F32), dma((3,))],
        compiler_params=pltpu.CompilerParams(vmem_limit_bytes=1_000_000),
    )(state, dual_out, misfit)
    return state, dual_out, misfit.reshape(())


def solution(mesh):
    in_specs = (
        P(None, "tile", None),
        P(None, None, "tile", None),
        P(None, None, "tile", None),
        P(None, "wave"),
        P(None, "wave", "tile", None),
        P(),
        P(),
        P(),
        P(),
        P(),
    )
    out_specs = (P(None, "tile", None), P(None, None, "tile", None), P())
    return jax.shard_map(
        per_device, mesh=mesh, in_specs=in_specs, out_specs=out_specs, check_vma=False
    )
```

```python
import functools

import jax
import jax.numpy as jnp
from jax import lax
from jax.experimental import pallas as pl
from jax.experimental.pallas import tpu as pltpu
from jax.sharding import PartitionSpec as P

MESH = pl.DeviceIdType.MESH
HALO = 8
TAPS = 17
F32 = jnp.float32
BF16 = jnp.bfloat16


def split_hi_lo(value):
    high = value.astype(BF16).astype(F32)
    return high, value - high


def group_size(count):
    size = 1
    while size * size < count:
        size *= 2
    return size if count % size == 0 else count


def kernel(
    tiles, waves, total_count,
    params_h, dual_h, jac_h, obs_h, response_h, psf_h, step_h, dstep_h, bound_h, clip_h,
    x_out, d_out, m_out,
    response, psf, step_size, dual_step, tv_bound, clip_bound, params, dual, jac, obs,
    wt, main_a, half_a, obs_f, obs_l, jac_n, jac_l, x_l, lhs, tot, proj, prod, grad_c,
    x_c, div_c, base_c, div_n, dpad, respad, psfpad, rt, rbf, rtb,
    jac_up, jac_dn, par_up, par_dn, dual_up, jac_hn,
    full0, edge0, full1, edge1, full0_in, up0_in, dn0_in, full1_in, up1_in, dn1_in,
    m_own, m_mid, m_group, m_cross,
    local, in_send, in_recv, f_recv, u_recv, d_recv,
    mg_send, mg_recv, mc_recv,
):
    npar, rows, ncol = params.shape
    images = jac.shape[0]
    stokes = images // npar
    nwave = response.shape[1]
    nimg = stokes * nwave
    width = -(-images // 8) * 8
    nrg = rows // HALO
    span = nrg + 2
    blk = HALO
    cols = ncol // blk
    unit = npar * blk
    me_t = lax.axis_index("tile")
    me_w = lax.axis_index("wave")
    up = lax.rem(me_t + tiles - 1, tiles)
    down = lax.rem(me_t + 1, tiles)
    gsize = group_size(tiles)
    ngroup = tiles // gsize
    my_group = me_t // gsize
    my_place = lax.rem(me_t, gsize)
    spin = [me_w] + [lax.rem(me_w + d, waves) for d in range(1, waves)]
    group_tiles = [me_t]
    group_tiles += [my_group * gsize + lax.rem(my_place + d, gsize) for d in range(1, gsize)]
    group_peers = [(t, w) for i, t in enumerate(group_tiles) for j, w in enumerate(spin) if i + j > 0]
    cross_peers = [
        (lax.rem(my_group + d, ngroup) * gsize + my_place, me_w) for d in range(1, ngroup)
    ]

    barrier = pltpu.get_barrier_semaphore()
    peers = [(up, me_w), (down, me_w)] + group_peers + cross_peers
    for peer in peers:
        pl.semaphore_signal(barrier, inc=1, device_id=peer, device_id_type=MESH)
    fetch = [
        pltpu.make_async_copy(jac_h, jac, local.at[0]),
        pltpu.make_async_copy(params_h, params, local.at[1]),
        pltpu.make_async_copy(dual_h, dual, local.at[2]),
        pltpu.make_async_copy(obs_h, obs, local.at[3]),
        pltpu.make_async_copy(psf_h, psf, local.at[4]),
        pltpu.make_async_copy(response_h, response, local.at[5]),
        pltpu.make_async_copy(step_h, step_size, local.at[6]),
        pltpu.make_async_copy(dstep_h, dual_step, local.at[7]),
        pltpu.make_async_copy(bound_h, tv_bound, local.at[8]),
        pltpu.make_async_copy(clip_h, clip_bound, local.at[9]),
    ]
    for copy in fetch:
        copy.start()

    lane = lax.broadcasted_iota(jnp.int32, (1, ncol), 1)
    group_bit = [(lane // (cols << b)) % 2 == 0 for b in range(3)]
    near = lane % cols < HALO

    def swap_blocks(parts):
        parts = list(parts)
        for b in range(3):
            k = 1 << b
            shift = cols * k
            for i in range(blk):
                if i & k:
                    continue
                one, two = parts[i], parts[i + k]
                parts[i] = jnp.where(group_bit[b], one, pltpu.roll(two, shift, 1))
                parts[i + k] = jnp.where(group_bit[b], pltpu.roll(one, ncol - shift, 1), two)
        return parts

    def image_rows(rg, b):
        return slice((rg * blk + b) * width, (rg * blk + b + 1) * width)

    def unit_rows(rg, b):
        return slice((rg * blk + b) * npar, (rg * blk + b + 1) * npar)

    def to_units(source, rg_from, target, rg_to):
        parts = swap_blocks([source[:, rg_from * HALO + r, :] for r in range(HALO)])
        for b in range(blk):
            target[unit_rows(rg_to, b), :] = parts[b]

    def to_blocks(source, height, rg_from, rg_to):
        for g in range(width // 8):
            at = g * 8 * height + rg_from * HALO
            parts = swap_blocks([source[pl.ds(at + r, 8, stride=height), :] for r in range(HALO)])
            for b in range(blk):
                at = (rg_to * blk + b) * width + g * 8
                jac_l[at:at + 8, :] = parts[b]

    def remote(src, dst, send, recv, peer):
        return pltpu.make_async_remote_copy(
            src_ref=src, dst_ref=dst, send_sem=send, recv_sem=recv,
            device_id=peer, device_id_type=MESH,
        )

    above, below = (up, me_w), (down, me_w)

    def unit_span(rg, count):
        return pl.ds(rg * unit, count * unit)

    top, last = pl.ds(0, HALO), pl.ds(rows - HALO, HALO)
    first = [
        remote(jac_h.at[:, last], jac_up, in_send.at[0], in_recv.at[0], below),
        remote(jac_h.at[:, top], jac_dn, in_send.at[1], in_recv.at[1], above),
        remote(params_h.at[:, last], par_up, in_send.at[2], in_recv.at[2], below),
        remote(params_h.at[:, top], par_dn, in_send.at[3], in_recv.at[3], above),
        remote(dual_h.at[0, :, last], dual_up, in_send.at[4], in_recv.at[4], below),
    ]
    fetch[4].wait()
    psfpad[...] = jnp.zeros_like(psfpad)
    psfpad[0:TAPS, 0:TAPS] = psf[...].astype(F32)
    taps = pltpu.roll(psfpad[...], ncol - HALO, 1)
    for tap in range(TAPS):
        line = jnp.broadcast_to(taps[tap:tap + 1, :], (cols, ncol))
        line = pltpu.roll(line, 0, 1, stride=1, stride_axis=0)
        side = jnp.where(near, pltpu.roll(line, ncol - cols, 1), pltpu.roll(line, cols, 1))
        for ref, value in ((main_a, line), (half_a, side)):
            value = jnp.where(lane < cols, value, 0.0)
            for b in range(3):
                value = value + pltpu.roll(value, cols << b, 1)
            ref[tap * cols:(tap + 1) * cols, :] = value
    wt[0, ncol:, :] = jnp.zeros((wt.shape[1] - ncol, 2 * ncol), BF16)
    for rg in range(1, span):
        for ro in range(nrg):
            if not 0 <= rg - ro <= 2:
                wt[rg, ro * ncol:(ro + 1) * ncol, :] = jnp.zeros((ncol, 2 * ncol), BF16)
    for delta in range(3):
        for r in range(HALO):
            for part, ref in ((0, main_a), (1, half_a)):
                value = jnp.zeros((cols, ncol), F32)
                for kr in range(HALO):
                    tap = delta * HALO + kr - r
                    if 0 <= tap < TAPS:
                        value = jnp.where(lane // cols == kr, ref[tap * cols:(tap + 1) * cols, :], value)
                value = value.astype(BF16)
                for ro in range(nrg):
                    at = ro * ncol + r * cols
                    wt[ro + delta, at:at + cols, part * ncol:(part + 1) * ncol] = value

    pl.semaphore_wait(barrier, len(peers))
    for copy in first:
        copy.start()

    jac_n[images * rows:, :] = jnp.zeros((jac_n.shape[0] - images * rows, ncol), F32)
    jac_hn[images * HALO:, :] = jnp.zeros((jac_hn.shape[0] - images * HALO, ncol), F32)
    edge1[...] = jnp.zeros_like(edge1)
    fetch[0].wait()
    for m in range(images):
        jac_n[m * rows:(m + 1) * rows, :] = jac[m].astype(F32)
    for rg in range(nrg):
        to_blocks(jac_n, rows, rg, rg + 1)
    fetch[1].wait()
    for rg in range(nrg):
        to_units(params, rg, x_c, rg + 1)
    fetch[2].wait()
    for copy in fetch[5:]:
        copy.wait()

    step = step_size[0]
    clip = clip_bound[0]
    bound = tv_bound[0]
    dstep = dual_step[0]

    def expand(rg):
        for b in range(blk):
            value = x_c[unit_rows(rg, b), :]
            at = (rg * blk + b) * width
            for s in range(stokes):
                x_l[at + s * npar:at + (s + 1) * npar, :] = value

    def build(rg):
        terms = [jac_l[image_rows(rg, b), :] * x_l[image_rows(rg, b), :] for b in range(blk)]
        for b in range(blk):
            side = jnp.where(near, terms[(b + 1) % blk], terms[(b + blk - 1) % blk])
            at = (rg * blk + b) * 2 * width
            for part, value in ((0, terms[b]), (1, side)):
                value = jnp.concatenate(split_hi_lo(value), axis=0).astype(BF16)
                lhs[at:at + 2 * width, part * ncol:(part + 1) * ncol] = value

    def forward(rg):
        window = lhs[rg * blk * 2 * width:(rg + 1) * blk * 2 * width, :]
        return lax.dot_general(
            window, wt[rg], (((1,), (1,)), ((), ())), preferred_element_type=F32
        )

    if width > images:
        for rg in range(span):
            for b in range(blk):
                at = (rg * blk + b) * width
                x_l[at + images:at + width, :] = jnp.zeros((width - images, ncol), F32)
    for rg in range(1, nrg + 1):
        expand(rg)
        build(rg)
    own = None
    for rg in range(1, nrg + 1):
        part = forward(rg)
        own = part if own is None else own + part
    tot[...] = own

    respad[...] = jnp.zeros_like(respad)
    respad[0:npar, 0:nwave] = response[...]
    rt[...] = jnp.zeros_like(rt)
    spread = respad[...]
    for s in range(stokes):
        shifted = spread if s == 0 else pltpu.roll(spread, s * nwave, 1)
        for part in range(3):
            at = part * width + s * npar
            rt[at:at + npar, :] = shifted[0:npar]
    full = rt[...]
    high, low = split_hi_lo(full)
    place = lax.broadcasted_iota(jnp.int32, full.shape, 0)
    rbf[...] = jnp.where(place < 2 * width, high, low).T.astype(BF16)
    rtb[...] = jnp.concatenate([high[0:width], low[0:width]], axis=0).astype(BF16)

    fetch[3].wait()
    obs_f[...] = obs[...].astype(F32).reshape(nimg * rows, ncol)
    def turn(g, carry):
        for rg in range(nrg):
            source = pl.multiple_of(g * 8 * rows, 8 * rows) + rg * HALO
            parts = swap_blocks([obs_f[pl.ds(source + r, 8, stride=rows), :] for r in range(HALO)])
            for b in range(blk):
                at = pl.multiple_of(b * nimg + g * 8, 8)
                obs_l[pl.ds(at, 8), rg * ncol:(rg + 1) * ncol] = parts[b]
        return carry

    lax.fori_loop(0, nimg // 8, turn, 0, unroll=4)
    for copy in first[:2]:
        copy.wait()
    for source, rg in ((jac_up, 0), (jac_dn, nrg + 1)):
        for m in range(images):
            jac_hn[m * HALO:(m + 1) * HALO, :] = source[m].astype(F32)
        to_blocks(jac_hn, HALO, 0, rg)
    for copy in first[2:4]:
        copy.wait()
    to_units(par_up, 0, x_c, 0)
    to_units(par_dn, 0, x_c, nrg + 1)
    zero_k = jnp.zeros((rbf.shape[1] - 3 * width, nrg * ncol), F32)

    for it in range(2):
        for rg in (0, nrg + 1) if it == 0 else range(span):
            expand(rg)
            build(rg)
        if it == 0:
            total = tot[...] + forward(0) + forward(nrg + 1)
        else:
            total = None
            for rg in range(span):
                part = forward(rg)
                total = part if total is None else total + part
        loss = jnp.zeros((8, nrg * ncol), F32)
        def respond(b):
            both = total[b * 2 * width:(b + 1) * 2 * width]
            bhi, blo = split_hi_lo(both[:width] + both[width:])
            stack = jnp.concatenate([bhi, blo, bhi, zero_k], axis=0).astype(BF16)
            return jnp.dot(rbf[...], stack, preferred_element_type=F32)

        def collect(b, held, before):
            both = jnp.dot(rtb[...], held, preferred_element_type=F32)
            both = both[:width] + both[width:]
            if b % 2 == 1:
                pair = jnp.concatenate([before, both], axis=0).astype(BF16)
                proj[(b - 1) * width:(b + 1) * width, :] = pair
            return both

        ahead = [respond(b) for b in range(4)]
        held_last = before = None
        for b in range(blk):
            if b + 4 < blk:
                ahead.append(respond(b + 4))
            blurred = ahead.pop(0)
            resid = blurred - obs_l[b * nimg:(b + 1) * nimg, :]
            held = jnp.clip(resid, -clip, clip)
            if it == 0:
                huber = held * (resid - 0.5 * held)
                loss = loss + jnp.sum(huber.reshape(nimg // 8, 8, nrg * ncol), axis=0)
            if b > 0:
                before = collect(b - 1, held_last, before)
            held_last = held.astype(BF16)
        collect(blk - 1, held_last, before)
        if it == 0:
            loss = sum(loss[:, i * ncol:(i + 1) * ncol] for i in range(nrg))

        def backward(rg):
            used = slice(max(rg - 2, 0) * ncol, min(rg + 1, nrg) * ncol)
            back = jnp.dot(proj[:, used], wt[rg, used, :], preferred_element_type=F32)
            mains = [back[b * width:(b + 1) * width, 0:ncol] for b in range(blk)]
            sides = [back[b * width:(b + 1) * width, ncol:] for b in range(blk)]
            for b in range(blk):
                along = mains[b] + jnp.where(near, sides[(b + blk - 1) % blk], sides[(b + 1) % blk])
                at = (rg * blk + b) * width
                prod[at:at + width, :] = jac_l[at:at + width, :] * along
                grad = None
                for s in range(stokes):
                    part = prod[at + s * npar:at + (s + 1) * npar, :]
                    grad = part if grad is None else grad + part
                grad_c[unit_rows(rg, b), :] = grad
        reach = 2 * unit if it == 0 else unit
        size = span * unit
        start = 0 if it == 0 else unit
        full_out, edge_out = (full0, edge0) if it == 0 else (full1, edge1)
        full_in, up_in, dn_in = (full0_in, up0_in, dn0_in) if it == 0 else (full1_in, up1_in, dn1_in)
        copies = []

        def send_edges():
            edge_out[0, 0:reach, :] = grad_c[0:reach, :].astype(BF16)
            edge_out[1, 0:reach, :] = grad_c[size - reach:, :].astype(BF16)
            for d in range(waves - 1, -1, -1):
                copies.append(remote(
                    edge_out.at[1], up_in.at[me_w], local.at[d], u_recv.at[it, d], (down, spin[d])
                ))
                copies.append(remote(
                    edge_out.at[0], dn_in.at[me_w], local.at[waves + d], d_recv.at[it, d], (up, spin[d])
                ))
            for copy in copies:
                copy.start()

        backward(0)
        backward(nrg + 1)
        if it == 1:
            send_edges()
        for rg in range(1, nrg + 1):
            backward(rg)
        if it == 0:
            send_edges()
        whole = grad_c[start:size - start, :].astype(BF16)
        full_out[...] = whole
        full_in[me_w] = whole
        for d in range(1, waves):
            copy = remote(full_out, full_in.at[me_w], local.at[2 * waves + d - 1], f_recv.at[it, d - 1], (me_t, spin[d]))
            copy.start()
            copies.append(copy)
        if it == 0:
            m_own[...] = loss
            slot = my_place * waves + me_w
            m_group[slot] = loss
            copies_g = [
                remote(m_own, m_group.at[slot], mg_send.at[d], mg_recv.at[d], peer)
                for d, peer in enumerate(group_peers)
            ]
            for copy in copies_g:
                copy.start()
            first[4].wait()
            now = params[...]
            d1 = pltpu.roll(now, ncol - 1, 2) - now
            d1 = jnp.clip(dual[1] + dstep * d1, -bound, bound)
            d_out[1] = d1
            dpad[:, HALO:HALO + rows, :] = now
            dpad[:, HALO + rows, :] = par_dn[:, 0, :]
            d0 = dpad[:, HALO + 1:HALO + 1 + rows, :] - now
            d0 = jnp.clip(dual[0] + dstep * d0, -bound, bound)
            d_out[0] = d0
            side = params[:, 0, :] - par_up[:, HALO - 1, :]
            side = jnp.clip(dual_up[:, HALO - 1, :] + dstep * side, -bound, bound)
            dpad[:, HALO - 1, :] = side
            dpad[:, HALO:HALO + rows, :] = d0
            div_n[...] = (d0 - dpad[:, HALO - 1:HALO - 1 + rows, :]) + (d1 - pltpu.roll(d1, 1, 2))
            for rg in range(nrg):
                to_units(div_n, rg, div_c, rg + 1)
            copies_v = [
                remote(
                    div_c.at[unit_span(nrg, 1)], div_c.at[unit_span(0, 1)],
                    in_send.at[5], in_recv.at[5], below,
                ),
                remote(
                    div_c.at[unit_span(1, 1)], div_c.at[unit_span(nrg + 1, 1)],
                    in_send.at[6], in_recv.at[6], above,
                ),
            ]
            for copy in copies_v:
                copy.start()
            for copy in copies_v:
                copy.wait()
            base_c[...] = x_c[...] + step * div_c[...]
        else:
            base_c[unit:size - unit, :] = x_c[unit:size - unit, :] + step * div_c[unit:size - unit, :]
            for copy in copies_g:
                copy.wait()
            total_m = m_group[0]
            for g in range(1, gsize * waves):
                total_m = total_m + m_group[g]
            m_mid[...] = total_m
            m_cross[my_group] = total_m
            copies_c = [
                remote(m_mid, m_cross.at[my_group], in_send.at[d], mc_recv.at[d], peer)
                for d, peer in enumerate(cross_peers)
            ]
            for copy in copies_c:
                copy.start()
            for copy in copies_c:
                copy.wait()
            tot_m = m_cross[0]
            for g in range(1, ngroup):
                tot_m = tot_m + m_cross[g]
            m_out[...] = jnp.full((8, ncol), jnp.sum(tot_m) / total_count, F32)
        for copy in copies:
            copy.wait()

        def added(ref, count):
            value = ref[0, 0:count, :].astype(F32)
            for w in range(1, waves):
                value = value + ref[w, 0:count, :].astype(F32)
            return value

        inner = added(full_in, size - 2 * start)
        top = inner[:reach] + added(up_in, reach)
        low = inner[size - 2 * start - reach:] + added(dn_in, reach)
        end = size - start
        x_c[start:start + reach, :] = base_c[start:start + reach, :] - step * top
        if end - start > 2 * reach:
            x_c[start + reach:end - reach, :] = (
                base_c[start + reach:end - reach, :] - step * inner[reach:end - start - reach]
            )
        x_c[end - reach:end, :] = base_c[end - reach:end, :] - step * low
    for rg in range(nrg):
        parts = swap_blocks([x_c[unit_rows(rg + 1, b), :] for b in range(blk)])
        for r in range(HALO):
            x_out[:, rg * HALO + r, :] = parts[r]


def hand_out(x, d, m, x_h, d_h, m_h, m_s, sem):
    copies = [pltpu.make_async_copy(x, x_h, sem.at[0]), pltpu.make_async_copy(d, d_h, sem.at[1])]
    for copy in copies:
        copy.start()
    m_s[0] = m[0, 0]
    copies.append(pltpu.make_async_copy(m_s, m_h, sem.at[2]))
    copies[2].start()
    for copy in copies:
        copy.wait()


def per_device(
    params, dual_in, jacobian, response, observed, psf, step_size, dual_step, tv_bound, clip_bound
):
    stokes, nwave, rows, ncol = observed.shape
    npar = params.shape[0]
    nimg = stokes * nwave
    images = stokes * npar
    width = -(-images // 8) * 8
    kdim = -(-3 * width // 128) * 128
    nrg = rows // HALO
    span = nrg + 2
    blk = HALO
    cols = ncol // blk
    unit = npar * blk
    edge = -(-unit // 16) * 16
    tiles = lax.axis_size("tile")
    waves = lax.axis_size("wave")
    total_count = float(nimg * waves * rows * tiles * ncol)
    gsize = group_size(tiles)
    ngroup = tiles // gsize
    vmem = pl.BlockSpec(memory_space=pltpu.VMEM)
    smem = pl.BlockSpec(memory_space=pltpu.SMEM)
    hbm = pl.BlockSpec(memory_space=pltpu.HBM)
    dma = pltpu.SemaphoreType.DMA
    state, dual_out, misfit = pl.pallas_call(
        functools.partial(kernel, tiles, waves, total_count),
        out_shape=(
            pltpu.VMEM((npar, rows, ncol), F32),
            pltpu.VMEM((2, npar, rows, ncol), F32),
            pltpu.VMEM((8, ncol), F32),
        ),
        in_specs=[hbm] * 10,
        out_specs=(vmem, vmem, vmem),
        scratch_shapes=[
            pltpu.VMEM(response.shape, F32),
            pltpu.VMEM(psf.shape, BF16),
            pltpu.SMEM((1,), F32),
            pltpu.SMEM((1,), F32),
            pltpu.SMEM((1,), F32),
            pltpu.SMEM((1,), F32),
            pltpu.VMEM((npar, rows, ncol), F32),
            pltpu.VMEM((2, npar, rows, ncol), F32),
            pltpu.VMEM((images, rows, ncol), BF16),
            pltpu.VMEM((nimg, rows, ncol), BF16),
            pltpu.VMEM((span, nrg * ncol, 2 * ncol), BF16),
            pltpu.VMEM((TAPS * cols, ncol), F32),
            pltpu.VMEM((TAPS * cols, ncol), F32),
            pltpu.VMEM((nimg * rows, ncol), F32),
            pltpu.VMEM((blk * nimg, nrg * ncol), F32),
            pltpu.VMEM((width * rows, ncol), F32),
            pltpu.VMEM((span * blk * width, ncol), F32),
            pltpu.VMEM((span * blk * width, ncol), F32),
            pltpu.VMEM((span * blk * 2 * width, 2 * ncol), BF16),
            pltpu.VMEM((blk * 2 * width, nrg * ncol), F32),
            pltpu.VMEM((blk * width, nrg * ncol), BF16),
            pltpu.VMEM((span * blk * width, ncol), F32),
            pltpu.VMEM((span * unit, ncol), F32),
            pltpu.VMEM((span * unit, ncol), F32),
            pltpu.VMEM((span * unit, ncol), F32),
            pltpu.VMEM((span * unit, ncol), F32),
            pltpu.VMEM((npar, rows, ncol), F32),
            pltpu.VMEM((npar, rows + 2 * HALO, ncol), F32),
            pltpu.VMEM((-(-npar // 8) * 8, nimg), F32),
            pltpu.VMEM((-(-TAPS // 8) * 8, ncol), F32),
            pltpu.VMEM((kdim, nimg), F32),
            pltpu.VMEM((nimg, kdim), BF16),
            pltpu.VMEM((2 * width, nimg), BF16),
            pltpu.VMEM((images, HALO, ncol), BF16),
            pltpu.VMEM((images, HALO, ncol), BF16),
            pltpu.VMEM((npar, HALO, ncol), F32),
            pltpu.VMEM((npar, HALO, ncol), F32),
            pltpu.VMEM((npar, HALO, ncol), F32),
            pltpu.VMEM((width * HALO, ncol), F32),
            pltpu.VMEM((span * unit, ncol), BF16),
            pltpu.VMEM((2, 2 * unit, ncol), BF16),
            pltpu.VMEM((nrg * unit, ncol), BF16),
            pltpu.VMEM((2, edge, ncol), BF16),
            pltpu.VMEM((waves, span * unit, ncol), BF16),
            pltpu.VMEM((waves, 2 * unit, ncol), BF16),
            pltpu.VMEM((waves, 2 * unit, ncol), BF16),
            pltpu.VMEM((waves, nrg * unit, ncol), BF16),
            pltpu.VMEM((waves, edge, ncol), BF16),
            pltpu.VMEM((waves, edge, ncol), BF16),
            pltpu.VMEM((8, ncol), F32),
            pltpu.VMEM((8, ncol), F32),
            pltpu.VMEM((gsize * waves, 8, ncol), F32),
            pltpu.VMEM((ngroup, 8, ncol), F32),
            dma((max(10, 3 * waves - 1),)),
            dma((max(7, ngroup - 1),)), dma((7,)),
            dma((2, max(1, waves - 1))),
            dma((2, waves)),
            dma((2, waves)),
            dma((max(1, gsize * waves - 1),)), dma((max(1, gsize * waves - 1),)),
            dma((max(1, ngroup - 1),)),
        ],
        compiler_params=pltpu.CompilerParams(
            collective_id=0, has_side_effects=True, vmem_limit_bytes=66_000_000
        ),
    )(
        params, dual_in, jacobian.reshape(images, rows, ncol),
        observed.reshape(nimg, rows, ncol), response, psf,
        step_size.reshape(1), dual_step.reshape(1), tv_bound.reshape(1), clip_bound.reshape(1),
    )
    state, dual_out, misfit = pl.pallas_call(
        hand_out,
        out_shape=(
            jax.ShapeDtypeStruct((npar, rows, ncol), F32),
            jax.ShapeDtypeStruct((2, npar, rows, ncol), F32),
            jax.ShapeDtypeStruct((1,), F32),
        ),
        in_specs=[vmem] * 3,
        out_specs=(hbm, hbm, hbm),
        scratch_shapes=[pltpu.SMEM((1,), F32), dma((3,))],
        compiler_params=pltpu.CompilerParams(vmem_limit_bytes=1_000_000),
    )(state, dual_out, misfit)
    return state, dual_out, misfit.reshape(())


def solution(mesh):
    in_specs = (
        P(None, "tile", None),
        P(None, None, "tile", None),
        P(None, None, "tile", None),
        P(None, "wave"),
        P(None, "wave", "tile", None),
        P(),
        P(),
        P(),
        P(),
        P(),
    )
    out_specs = (P(None, "tile", None), P(None, None, "tile", None), P())
    return jax.shard_map(
        per_device, mesh=mesh, in_specs=in_specs, out_specs=out_specs, check_vma=False
    )
```

```python
import functools

import jax
import jax.numpy as jnp
from jax import lax
from jax.experimental import pallas as pl
from jax.experimental.pallas import tpu as pltpu
from jax.sharding import PartitionSpec as P

MESH = pl.DeviceIdType.MESH
HALO = 8
TAPS = 17
F32 = jnp.float32
BF16 = jnp.bfloat16


def split_hi_lo(value):
    high = value.astype(BF16).astype(F32)
    return high, value - high


def group_size(count):
    size = 1
    while size * size < count:
        size *= 2
    return size if count % size == 0 else count


def kernel(
    tiles, waves, total_count,
    params_h, dual_h, jac_h, obs_h, response_h, psf_h, step_h, dstep_h, bound_h, clip_h,
    x_out, d_out, m_out,
    response, psf, step_size, dual_step, tv_bound, clip_bound, params, dual, jac, obs,
    wt, main_a, half_a, obs_f, obs_l, jac_n, jac_l, x_l, lhs, tot, proj, prod, grad_c,
    x_c, div_c, base_c, div_n, dpad, respad, psfpad, rt, rbf, rtb,
    jac_up, jac_dn, par_up, par_dn, dual_up, jac_hn,
    full0, edge0, full1, edge1, full0_in, up0_in, dn0_in, full1_in, up1_in, dn1_in,
    m_own, m_mid, m_group, m_cross,
    local, in_send, in_recv, f_recv, u_recv, d_recv,
    mg_send, mg_recv, mc_recv,
):
    npar, rows, ncol = params.shape
    images = jac.shape[0]
    stokes = images // npar
    nwave = response.shape[1]
    nimg = stokes * nwave
    width = -(-images // 8) * 8
    nrg = rows // HALO
    span = nrg + 2
    blk = HALO
    cols = ncol // blk
    unit = npar * blk
    me_t = lax.axis_index("tile")
    me_w = lax.axis_index("wave")
    up = lax.rem(me_t + tiles - 1, tiles)
    down = lax.rem(me_t + 1, tiles)
    gsize = group_size(tiles)
    ngroup = tiles // gsize
    my_group = me_t // gsize
    my_place = lax.rem(me_t, gsize)
    spin = [me_w] + [lax.rem(me_w + d, waves) for d in range(1, waves)]
    group_tiles = [me_t]
    group_tiles += [my_group * gsize + lax.rem(my_place + d, gsize) for d in range(1, gsize)]
    group_peers = [(t, w) for i, t in enumerate(group_tiles) for j, w in enumerate(spin) if i + j > 0]
    cross_peers = [
        (lax.rem(my_group + d, ngroup) * gsize + my_place, me_w) for d in range(1, ngroup)
    ]

    barrier = pltpu.get_barrier_semaphore()
    peers = [(up, me_w), (down, me_w)] + group_peers + cross_peers
    for peer in peers:
        pl.semaphore_signal(barrier, inc=1, device_id=peer, device_id_type=MESH)
    fetch = [
        pltpu.make_async_copy(jac_h, jac, local.at[0]),
        pltpu.make_async_copy(params_h, params, local.at[1]),
        pltpu.make_async_copy(dual_h, dual, local.at[2]),
        pltpu.make_async_copy(obs_h, obs, local.at[3]),
        pltpu.make_async_copy(psf_h, psf, local.at[4]),
        pltpu.make_async_copy(response_h, response, local.at[5]),
        pltpu.make_async_copy(step_h, step_size, local.at[6]),
        pltpu.make_async_copy(dstep_h, dual_step, local.at[7]),
        pltpu.make_async_copy(bound_h, tv_bound, local.at[8]),
        pltpu.make_async_copy(clip_h, clip_bound, local.at[9]),
    ]
    for n in (4, 0, 1, 5, 6, 7, 8, 9):
        fetch[n].start()

    lane = lax.broadcasted_iota(jnp.int32, (1, ncol), 1)
    group_bit = [(lane // (cols << b)) % 2 == 0 for b in range(3)]
    near = lane % cols < HALO

    def swap_blocks(parts):
        parts = list(parts)
        for b in range(3):
            k = 1 << b
            shift = cols * k
            for i in range(blk):
                if i & k:
                    continue
                one, two = parts[i], parts[i + k]
                parts[i] = jnp.where(group_bit[b], one, pltpu.roll(two, shift, 1))
                parts[i + k] = jnp.where(group_bit[b], pltpu.roll(one, ncol - shift, 1), two)
        return parts

    def image_rows(rg, b):
        return slice((rg * blk + b) * width, (rg * blk + b + 1) * width)

    def unit_rows(rg, b):
        return slice((rg * blk + b) * npar, (rg * blk + b + 1) * npar)

    def to_units(source, rg_from, target, rg_to):
        parts = swap_blocks([source[:, rg_from * HALO + r, :] for r in range(HALO)])
        for b in range(blk):
            target[unit_rows(rg_to, b), :] = parts[b]

    def to_blocks(source, height, rg_from, rg_to):
        for g in range(width // 8):
            at = g * 8 * height + rg_from * HALO
            parts = swap_blocks([source[pl.ds(at + r, 8, stride=height), :] for r in range(HALO)])
            for b in range(blk):
                at = (rg_to * blk + b) * width + g * 8
                jac_l[at:at + 8, :] = parts[b]

    def remote(src, dst, send, recv, peer):
        return pltpu.make_async_remote_copy(
            src_ref=src, dst_ref=dst, send_sem=send, recv_sem=recv,
            device_id=peer, device_id_type=MESH,
        )

    above, below = (up, me_w), (down, me_w)

    def unit_span(rg, count):
        return pl.ds(rg * unit, count * unit)

    top, last = pl.ds(0, HALO), pl.ds(rows - HALO, HALO)
    first = [
        remote(jac_h.at[:, last], jac_up, in_send.at[0], in_recv.at[0], below),
        remote(jac_h.at[:, top], jac_dn, in_send.at[1], in_recv.at[1], above),
        remote(params_h.at[:, last], par_up, in_send.at[2], in_recv.at[2], below),
        remote(params_h.at[:, top], par_dn, in_send.at[3], in_recv.at[3], above),
        remote(dual_h.at[0, :, last], dual_up, in_send.at[4], in_recv.at[4], below),
    ]
    fetch[4].wait()
    psfpad[...] = jnp.zeros_like(psfpad)
    psfpad[0:TAPS, 0:TAPS] = psf[...].astype(F32)
    taps = pltpu.roll(psfpad[...], ncol - HALO, 1)
    for tap in range(TAPS):
        line = jnp.broadcast_to(taps[tap:tap + 1, :], (cols, ncol))
        line = pltpu.roll(line, 0, 1, stride=1, stride_axis=0)
        side = jnp.where(near, pltpu.roll(line, ncol - cols, 1), pltpu.roll(line, cols, 1))
        for ref, value in ((main_a, line), (half_a, side)):
            value = jnp.where(lane < cols, value, 0.0)
            for b in range(3):
                value = value + pltpu.roll(value, cols << b, 1)
            ref[tap * cols:(tap + 1) * cols, :] = value
    wt[0, ncol:, :] = jnp.zeros((wt.shape[1] - ncol, 2 * ncol), BF16)
    for rg in range(1, span):
        for ro in range(nrg):
            if not 0 <= rg - ro <= 2:
                wt[rg, ro * ncol:(ro + 1) * ncol, :] = jnp.zeros((ncol, 2 * ncol), BF16)
    for delta in range(3):
        for r in range(HALO):
            for part, ref in ((0, main_a), (1, half_a)):
                value = jnp.zeros((cols, ncol), F32)
                for kr in range(HALO):
                    tap = delta * HALO + kr - r
                    if 0 <= tap < TAPS:
                        value = jnp.where(lane // cols == kr, ref[tap * cols:(tap + 1) * cols, :], value)
                value = value.astype(BF16)
                for ro in range(nrg):
                    at = ro * ncol + r * cols
                    wt[ro + delta, at:at + cols, part * ncol:(part + 1) * ncol] = value

    pl.semaphore_wait(barrier, len(peers))
    for copy in first:
        copy.start()
    for n in (2, 3):
        fetch[n].start()

    jac_n[images * rows:, :] = jnp.zeros((jac_n.shape[0] - images * rows, ncol), F32)
    jac_hn[images * HALO:, :] = jnp.zeros((jac_hn.shape[0] - images * HALO, ncol), F32)
    edge1[...] = jnp.zeros_like(edge1)
    fetch[0].wait()
    for m in range(images):
        jac_n[m * rows:(m + 1) * rows, :] = jac[m].astype(F32)
    for rg in range(nrg):
        to_blocks(jac_n, rows, rg, rg + 1)
    fetch[1].wait()
    for rg in range(nrg):
        to_units(params, rg, x_c, rg + 1)
    fetch[2].wait()
    for copy in fetch[5:]:
        copy.wait()

    step = step_size[0]
    clip = clip_bound[0]
    bound = tv_bound[0]
    dstep = dual_step[0]

    def expand(rg):
        for b in range(blk):
            value = x_c[unit_rows(rg, b), :]
            at = (rg * blk + b) * width
            for s in range(stokes):
                x_l[at + s * npar:at + (s + 1) * npar, :] = value

    def build(rg):
        terms = [jac_l[image_rows(rg, b), :] * x_l[image_rows(rg, b), :] for b in range(blk)]
        for b in range(blk):
            side = jnp.where(near, terms[(b + 1) % blk], terms[(b + blk - 1) % blk])
            at = (rg * blk + b) * 2 * width
            for part, value in ((0, terms[b]), (1, side)):
                value = jnp.concatenate(split_hi_lo(value), axis=0).astype(BF16)
                lhs[at:at + 2 * width, part * ncol:(part + 1) * ncol] = value

    def forward(rg):
        window = lhs[rg * blk * 2 * width:(rg + 1) * blk * 2 * width, :]
        return lax.dot_general(
            window, wt[rg], (((1,), (1,)), ((), ())), preferred_element_type=F32
        )

    if width > images:
        for rg in range(span):
            for b in range(blk):
                at = (rg * blk + b) * width
                x_l[at + images:at + width, :] = jnp.zeros((width - images, ncol), F32)
    for rg in range(1, nrg + 1):
        expand(rg)
        build(rg)
    own = None
    for rg in range(1, nrg + 1):
        part = forward(rg)
        own = part if own is None else own + part
    tot[...] = own

    respad[...] = jnp.zeros_like(respad)
    respad[0:npar, 0:nwave] = response[...]
    rt[...] = jnp.zeros_like(rt)
    spread = respad[...]
    for s in range(stokes):
        shifted = spread if s == 0 else pltpu.roll(spread, s * nwave, 1)
        for part in range(3):
            at = part * width + s * npar
            rt[at:at + npar, :] = shifted[0:npar]
    full = rt[...]
    high, low = split_hi_lo(full)
    place = lax.broadcasted_iota(jnp.int32, full.shape, 0)
    rbf[...] = jnp.where(place < 2 * width, high, low).T.astype(BF16)
    rtb[...] = jnp.concatenate([high[0:width], low[0:width]], axis=0).astype(BF16)

    fetch[3].wait()
    obs_f[...] = obs[...].astype(F32).reshape(nimg * rows, ncol)
    def turn(g, carry):
        for rg in range(nrg):
            source = pl.multiple_of(g * 8 * rows, 8 * rows) + rg * HALO
            parts = swap_blocks([obs_f[pl.ds(source + r, 8, stride=rows), :] for r in range(HALO)])
            for b in range(blk):
                at = pl.multiple_of(b * nimg + g * 8, 8)
                obs_l[pl.ds(at, 8), rg * ncol:(rg + 1) * ncol] = parts[b]
        return carry

    lax.fori_loop(0, nimg // 8, turn, 0, unroll=4)
    for copy in first[:2]:
        copy.wait()
    for source, rg in ((jac_up, 0), (jac_dn, nrg + 1)):
        for m in range(images):
            jac_hn[m * HALO:(m + 1) * HALO, :] = source[m].astype(F32)
        to_blocks(jac_hn, HALO, 0, rg)
    for copy in first[2:4]:
        copy.wait()
    to_units(par_up, 0, x_c, 0)
    to_units(par_dn, 0, x_c, nrg + 1)
    zero_k = jnp.zeros((rbf.shape[1] - 3 * width, nrg * ncol), F32)

    for it in range(2):
        for rg in (0, nrg + 1) if it == 0 else range(span):
            expand(rg)
            build(rg)
        if it == 0:
            total = tot[...] + forward(0) + forward(nrg + 1)
        else:
            total = None
            for rg in range(span):
                part = forward(rg)
                total = part if total is None else total + part
        loss = jnp.zeros((8, nrg * ncol), F32)
        def respond(b):
            both = total[b * 2 * width:(b + 1) * 2 * width]
            bhi, blo = split_hi_lo(both[:width] + both[width:])
            stack = jnp.concatenate([bhi, blo, bhi, zero_k], axis=0).astype(BF16)
            return jnp.dot(rbf[...], stack, preferred_element_type=F32)

        def collect(b, held, before):
            both = jnp.dot(rtb[...], held, preferred_element_type=F32)
            both = both[:width] + both[width:]
            if b % 2 == 1:
                pair = jnp.concatenate([before, both], axis=0).astype(BF16)
                proj[(b - 1) * width:(b + 1) * width, :] = pair
            return both

        ahead = [respond(b) for b in range(4)]
        held_last = before = None
        for b in range(blk):
            if b + 4 < blk:
                ahead.append(respond(b + 4))
            blurred = ahead.pop(0)
            resid = blurred - obs_l[b * nimg:(b + 1) * nimg, :]
            held = jnp.clip(resid, -clip, clip)
            if it == 0:
                huber = held * (resid - 0.5 * held)
                loss = loss + jnp.sum(huber.reshape(nimg // 8, 8, nrg * ncol), axis=0)
            if b > 0:
                before = collect(b - 1, held_last, before)
            held_last = held.astype(BF16)
        collect(blk - 1, held_last, before)
        if it == 0:
            loss = sum(loss[:, i * ncol:(i + 1) * ncol] for i in range(nrg))

        def backward(rg):
            used = slice(max(rg - 2, 0) * ncol, min(rg + 1, nrg) * ncol)
            back = jnp.dot(proj[:, used], wt[rg, used, :], preferred_element_type=F32)
            mains = [back[b * width:(b + 1) * width, 0:ncol] for b in range(blk)]
            sides = [back[b * width:(b + 1) * width, ncol:] for b in range(blk)]
            for b in range(blk):
                along = mains[b] + jnp.where(near, sides[(b + blk - 1) % blk], sides[(b + 1) % blk])
                at = (rg * blk + b) * width
                prod[at:at + width, :] = jac_l[at:at + width, :] * along
                grad = None
                for s in range(stokes):
                    part = prod[at + s * npar:at + (s + 1) * npar, :]
                    grad = part if grad is None else grad + part
                grad_c[unit_rows(rg, b), :] = grad
        reach = 2 * unit if it == 0 else unit
        size = span * unit
        start = 0 if it == 0 else unit
        full_out, edge_out = (full0, edge0) if it == 0 else (full1, edge1)
        full_in, up_in, dn_in = (full0_in, up0_in, dn0_in) if it == 0 else (full1_in, up1_in, dn1_in)
        copies = []

        def send_edges():
            edge_out[0, 0:reach, :] = grad_c[0:reach, :].astype(BF16)
            edge_out[1, 0:reach, :] = grad_c[size - reach:, :].astype(BF16)
            for d in range(waves - 1, -1, -1):
                copies.append(remote(
                    edge_out.at[1], up_in.at[me_w], local.at[d], u_recv.at[it, d], (down, spin[d])
                ))
                copies.append(remote(
                    edge_out.at[0], dn_in.at[me_w], local.at[waves + d], d_recv.at[it, d], (up, spin[d])
                ))
            for copy in copies:
                copy.start()

        backward(0)
        backward(nrg + 1)
        if it == 1:
            send_edges()
        for rg in range(1, nrg + 1):
            backward(rg)
        if it == 0:
            send_edges()
        whole = grad_c[start:size - start, :].astype(BF16)
        full_out[...] = whole
        full_in[me_w] = whole
        for d in range(1, waves):
            copy = remote(full_out, full_in.at[me_w], local.at[2 * waves + d - 1], f_recv.at[it, d - 1], (me_t, spin[d]))
            copy.start()
            copies.append(copy)
        if it == 0:
            m_own[...] = loss
            slot = my_place * waves + me_w
            m_group[slot] = loss
            copies_g = [
                remote(m_own, m_group.at[slot], mg_send.at[d], mg_recv.at[d], peer)
                for d, peer in enumerate(group_peers)
            ]
            for copy in copies_g:
                copy.start()
            first[4].wait()
            now = params[...]
            d1 = pltpu.roll(now, ncol - 1, 2) - now
            d1 = jnp.clip(dual[1] + dstep * d1, -bound, bound)
            d_out[1] = d1
            dpad[:, HALO:HALO + rows, :] = now
            dpad[:, HALO + rows, :] = par_dn[:, 0, :]
            d0 = dpad[:, HALO + 1:HALO + 1 + rows, :] - now
            d0 = jnp.clip(dual[0] + dstep * d0, -bound, bound)
            d_out[0] = d0
            side = params[:, 0, :] - par_up[:, HALO - 1, :]
            side = jnp.clip(dual_up[:, HALO - 1, :] + dstep * side, -bound, bound)
            dpad[:, HALO - 1, :] = side
            dpad[:, HALO:HALO + rows, :] = d0
            div_n[...] = (d0 - dpad[:, HALO - 1:HALO - 1 + rows, :]) + (d1 - pltpu.roll(d1, 1, 2))
            for rg in range(nrg):
                to_units(div_n, rg, div_c, rg + 1)
            copies_v = [
                remote(
                    div_c.at[unit_span(nrg, 1)], div_c.at[unit_span(0, 1)],
                    in_send.at[5], in_recv.at[5], below,
                ),
                remote(
                    div_c.at[unit_span(1, 1)], div_c.at[unit_span(nrg + 1, 1)],
                    in_send.at[6], in_recv.at[6], above,
                ),
            ]
            for copy in copies_v:
                copy.start()
            for copy in copies_v:
                copy.wait()
            base_c[...] = x_c[...] + step * div_c[...]
        else:
            base_c[unit:size - unit, :] = x_c[unit:size - unit, :] + step * div_c[unit:size - unit, :]
            for copy in copies_g:
                copy.wait()
            total_m = m_group[0]
            for g in range(1, gsize * waves):
                total_m = total_m + m_group[g]
            m_mid[...] = total_m
            m_cross[my_group] = total_m
            copies_c = [
                remote(m_mid, m_cross.at[my_group], in_send.at[d], mc_recv.at[d], peer)
                for d, peer in enumerate(cross_peers)
            ]
            for copy in copies_c:
                copy.start()
            for copy in copies_c:
                copy.wait()
            tot_m = m_cross[0]
            for g in range(1, ngroup):
                tot_m = tot_m + m_cross[g]
            m_out[...] = jnp.full((8, ncol), jnp.sum(tot_m) / total_count, F32)
        for copy in copies:
            copy.wait()

        def added(ref, count):
            value = ref[0, 0:count, :].astype(F32)
            for w in range(1, waves):
                value = value + ref[w, 0:count, :].astype(F32)
            return value

        inner = added(full_in, size - 2 * start)
        top = inner[:reach] + added(up_in, reach)
        low = inner[size - 2 * start - reach:] + added(dn_in, reach)
        end = size - start
        x_c[start:start + reach, :] = base_c[start:start + reach, :] - step * top
        if end - start > 2 * reach:
            x_c[start + reach:end - reach, :] = (
                base_c[start + reach:end - reach, :] - step * inner[reach:end - start - reach]
            )
        x_c[end - reach:end, :] = base_c[end - reach:end, :] - step * low
    for rg in range(nrg):
        parts = swap_blocks([x_c[unit_rows(rg + 1, b), :] for b in range(blk)])
        for r in range(HALO):
            x_out[:, rg * HALO + r, :] = parts[r]


def hand_out(x, d, m, x_h, d_h, m_h, m_s, sem):
    copies = [pltpu.make_async_copy(x, x_h, sem.at[0]), pltpu.make_async_copy(d, d_h, sem.at[1])]
    for copy in copies:
        copy.start()
    m_s[0] = m[0, 0]
    copies.append(pltpu.make_async_copy(m_s, m_h, sem.at[2]))
    copies[2].start()
    for copy in copies:
        copy.wait()


def per_device(
    params, dual_in, jacobian, response, observed, psf, step_size, dual_step, tv_bound, clip_bound
):
    stokes, nwave, rows, ncol = observed.shape
    npar = params.shape[0]
    nimg = stokes * nwave
    images = stokes * npar
    width = -(-images // 8) * 8
    kdim = -(-3 * width // 128) * 128
    nrg = rows // HALO
    span = nrg + 2
    blk = HALO
    cols = ncol // blk
    unit = npar * blk
    edge = -(-unit // 16) * 16
    tiles = lax.axis_size("tile")
    waves = lax.axis_size("wave")
    total_count = float(nimg * waves * rows * tiles * ncol)
    gsize = group_size(tiles)
    ngroup = tiles // gsize
    vmem = pl.BlockSpec(memory_space=pltpu.VMEM)
    smem = pl.BlockSpec(memory_space=pltpu.SMEM)
    hbm = pl.BlockSpec(memory_space=pltpu.HBM)
    dma = pltpu.SemaphoreType.DMA
    state, dual_out, misfit = pl.pallas_call(
        functools.partial(kernel, tiles, waves, total_count),
        out_shape=(
            pltpu.VMEM((npar, rows, ncol), F32),
            pltpu.VMEM((2, npar, rows, ncol), F32),
            pltpu.VMEM((8, ncol), F32),
        ),
        in_specs=[hbm] * 10,
        out_specs=(vmem, vmem, vmem),
        scratch_shapes=[
            pltpu.VMEM(response.shape, F32),
            pltpu.VMEM(psf.shape, BF16),
            pltpu.SMEM((1,), F32),
            pltpu.SMEM((1,), F32),
            pltpu.SMEM((1,), F32),
            pltpu.SMEM((1,), F32),
            pltpu.VMEM((npar, rows, ncol), F32),
            pltpu.VMEM((2, npar, rows, ncol), F32),
            pltpu.VMEM((images, rows, ncol), BF16),
            pltpu.VMEM((nimg, rows, ncol), BF16),
            pltpu.VMEM((span, nrg * ncol, 2 * ncol), BF16),
            pltpu.VMEM((TAPS * cols, ncol), F32),
            pltpu.VMEM((TAPS * cols, ncol), F32),
            pltpu.VMEM((nimg * rows, ncol), F32),
            pltpu.VMEM((blk * nimg, nrg * ncol), F32),
            pltpu.VMEM((width * rows, ncol), F32),
            pltpu.VMEM((span * blk * width, ncol), F32),
            pltpu.VMEM((span * blk * width, ncol), F32),
            pltpu.VMEM((span * blk * 2 * width, 2 * ncol), BF16),
            pltpu.VMEM((blk * 2 * width, nrg * ncol), F32),
            pltpu.VMEM((blk * width, nrg * ncol), BF16),
            pltpu.VMEM((span * blk * width, ncol), F32),
            pltpu.VMEM((span * unit, ncol), F32),
            pltpu.VMEM((span * unit, ncol), F32),
            pltpu.VMEM((span * unit, ncol), F32),
            pltpu.VMEM((span * unit, ncol), F32),
            pltpu.VMEM((npar, rows, ncol), F32),
            pltpu.VMEM((npar, rows + 2 * HALO, ncol), F32),
            pltpu.VMEM((-(-npar // 8) * 8, nimg), F32),
            pltpu.VMEM((-(-TAPS // 8) * 8, ncol), F32),
            pltpu.VMEM((kdim, nimg), F32),
            pltpu.VMEM((nimg, kdim), BF16),
            pltpu.VMEM((2 * width, nimg), BF16),
            pltpu.VMEM((images, HALO, ncol), BF16),
            pltpu.VMEM((images, HALO, ncol), BF16),
            pltpu.VMEM((npar, HALO, ncol), F32),
            pltpu.VMEM((npar, HALO, ncol), F32),
            pltpu.VMEM((npar, HALO, ncol), F32),
            pltpu.VMEM((width * HALO, ncol), F32),
            pltpu.VMEM((span * unit, ncol), BF16),
            pltpu.VMEM((2, 2 * unit, ncol), BF16),
            pltpu.VMEM((nrg * unit, ncol), BF16),
            pltpu.VMEM((2, edge, ncol), BF16),
            pltpu.VMEM((waves, span * unit, ncol), BF16),
            pltpu.VMEM((waves, 2 * unit, ncol), BF16),
            pltpu.VMEM((waves, 2 * unit, ncol), BF16),
            pltpu.VMEM((waves, nrg * unit, ncol), BF16),
            pltpu.VMEM((waves, edge, ncol), BF16),
            pltpu.VMEM((waves, edge, ncol), BF16),
            pltpu.VMEM((8, ncol), F32),
            pltpu.VMEM((8, ncol), F32),
            pltpu.VMEM((gsize * waves, 8, ncol), F32),
            pltpu.VMEM((ngroup, 8, ncol), F32),
            dma((max(10, 3 * waves - 1),)),
            dma((max(7, ngroup - 1),)), dma((7,)),
            dma((2, max(1, waves - 1))),
            dma((2, waves)),
            dma((2, waves)),
            dma((max(1, gsize * waves - 1),)), dma((max(1, gsize * waves - 1),)),
            dma((max(1, ngroup - 1),)),
        ],
        compiler_params=pltpu.CompilerParams(
            collective_id=0, has_side_effects=True, vmem_limit_bytes=66_000_000
        ),
    )(
        params, dual_in, jacobian.reshape(images, rows, ncol),
        observed.reshape(nimg, rows, ncol), response, psf,
        step_size.reshape(1), dual_step.reshape(1), tv_bound.reshape(1), clip_bound.reshape(1),
    )
    state, dual_out, misfit = pl.pallas_call(
        hand_out,
        out_shape=(
            jax.ShapeDtypeStruct((npar, rows, ncol), F32),
            jax.ShapeDtypeStruct((2, npar, rows, ncol), F32),
            jax.ShapeDtypeStruct((1,), F32),
        ),
        in_specs=[vmem] * 3,
        out_specs=(hbm, hbm, hbm),
        scratch_shapes=[pltpu.SMEM((1,), F32), dma((3,))],
        compiler_params=pltpu.CompilerParams(vmem_limit_bytes=1_000_000),
    )(state, dual_out, misfit)
    return state, dual_out, misfit.reshape(())


def solution(mesh):
    in_specs = (
        P(None, "tile", None),
        P(None, None, "tile", None),
        P(None, None, "tile", None),
        P(None, "wave"),
        P(None, "wave", "tile", None),
        P(),
        P(),
        P(),
        P(),
        P(),
    )
    out_specs = (P(None, "tile", None), P(None, None, "tile", None), P())
    return jax.shard_map(
        per_device, mesh=mesh, in_specs=in_specs, out_specs=out_specs, check_vma=False
    )
```
